128 devices in a mesh: req: 16 (over z, x), head: 8 (over y, core).
Axes of the slice: x: 4, y: 4, z: 4, core: 2. Of those that a mesh axis runs over, the one named last changes fastest.
Arguments:
- hidden_in: bfloat16 [16384, 2048], P(('req', 'head')), may hold values from -1.5 to 1.5
- attn_gain: float32 [2048], replicated, may hold values from 0.1 to 1.9
- query_weight: bfloat16 [2048, 3072], P(None, 'head'), may hold values from -0.25 to 0.25
- latent_weight: bfloat16 [2048, 512], replicated, may hold values from -0.125 to 0.125
- rope_key_weight: bfloat16 [64, 2048], replicated, may hold values from -0.125 to 0.125
- latent_gain: float32 [512], replicated, may hold values from 0.1 to 1.9
- kv_up_weight: bfloat16 [512, 4096], P(None, 'head'), may hold values from -0.25 to 0.25
- out_weight: bfloat16 [2048, 2048], P('head'), may hold values from -0.5 to 0.5
- pool_latent: bfloat16 [256, 128, 512], P('req'), may hold values from -1.6953125 to 1.6953125
- pool_rope: bfloat16 [256, 64, 128], P('req'), may hold values from -1.6953125 to 1.6953125
- page_table: int32 [16, 16], P('req'), may hold values from 0 to 15, each once within a row
- cache_len: int32 [16], P('req'), may hold values from 1 to 2048, 16384 in all
- post_gain: float32 [2048], replicated, may hold values from 0.1 to 1.9
- router_weight: bfloat16 [2048, 64], replicated, may hold values from -0.125 to 0.125
- routes: int32 [16384, 6], P(('req', 'head')), may hold values from 0 to 63, all different within a row; in each aligned block of 128 rows (0 to 127, 128 to 255, ...) at most 14 rows name the same one
- shared_gate_up: bfloat16 [2, 2048, 2816], P(None, None, 'head'), may hold values from -0.125 to 0.125
- shared_down: bfloat16 [2816, 2048], P('head'), may hold values from -0.109375 to 0.109375
- expert_gate_up: bfloat16 [128, 2, 2048, 704], P(('req', 'head')), may hold values from -0.125 to 0.125
- expert_down: bfloat16 [128, 704, 2048], P(('req', 'head')), may hold values from -1.25 to 1.25
Outputs:
- hidden_out: bfloat16 [16384, 2048], P(('req', 'head'))
- latent_new: bfloat16 [16384, 512], P(('req', 'head'))
- rope_new: bfloat16 [64, 16384], P(None, ('req', 'head'))
The draws below stay inside these ranges and needn't reach their ends.
Inputs may be any that keep to these rules, and one draw needn't show every extreme that they name: `routes`: in each aligned block of 128 rows (the rows of one device), no expert is named by more than 14 rows, a bound that some block reaches; the 6 entries of a row differ. Each row is a permutation; entry p of row r is the page, row r * 16 + page_table[r, p] of the pools, that holds cached positions p * 128 to (p + 1) * 128 - 1 of request r. `cache_len`: the lengths sum to 16384, and one of them is 2048.
All inputs are finite; a program needn't handle non-finite values. No bound on the sum of `cache_len` on one device may be relied on, other than what follows from the above.
Results may differ from the reference program's by a relative error of at most 0.03.
Values may be sent and summed in bfloat16 or wider, within the bound.
A program may use at most 128 MiB of HBM per device.

```python
import math
import jax
import jax.numpy as jnp
import numpy as np
from jax import lax

D = 2048
HEADS = 16
HEAD_NOPE = 128
ROPE = 64
VDIM = 128
LATENT = 512
EXPERTS = 64
FFE = 1408
SHARED_FF = 2816
TOP = 6
NEW_TOK = 1024
MAX_CACHE = 2048
PAGE = 128
REQS = 16
TOKENS = 16384
TOK_DEV = 128
PAGES = 16
CAP = 14
N_HEAD = 8


def level_of(own_key, dims, split, low, high):
    gain = 1.0
    for position, parts in split:
        steps = jax.random.uniform(jax.random.fold_in(jax.random.fold_in(own_key, 6), position), (parts,), jnp.float32, low / len(split), high / len(split))
        gain = gain * jnp.repeat(jnp.exp(steps), dims[position] // parts).reshape((-1,) + (1,) * (len(dims) - 1 - position))
    return gain


def split_up(amount, total, limit, lean):
    portions = [(1 << 20) // math.isqrt(rank ** lean) + 1 for rank in range(2, amount + 1)]
    rest, given = total - limit - (amount - 1), [1] * (amount - 1)
    while rest > 0:
        candidates = [i for i in range(amount - 1) if given[i] < limit]
        mass, budget = sum([portions[i] for i in candidates]), rest
        for i in candidates:
            more = min(limit - given[i], max(1, budget * portions[i] // mass), rest)
            given[i] = given[i] + more
            rest = rest - more
    return np.array([limit] + given)


def uneven(rng, number_of, total, bound, skew):
    if number_of == 2:
        one = jax.random.randint(rng, (), max(1, total - bound), min(bound, total - 1) + 1)
        return jnp.stack([one, total - one])
    tallies = jnp.asarray(split_up(number_of, total, bound, skew), jnp.int32)
    twos = (number_of - 1) // 2
    source_of, sink = tallies[1:1 + 2 * twos:2], tallies[2:2 + 2 * twos:2]
    margin = jnp.minimum(source_of - 1, bound - sink)
    moved = jax.random.randint(jax.random.fold_in(rng, 1), (twos,), 0, 1 << 20) % (margin + 1)
    tallies = tallies.at[1:1 + 2 * twos:2].set(source_of - moved).at[2:2 + 2 * twos:2].set(sink + moved)
    return tallies[jax.random.permutation(jax.random.fold_in(rng, 2), number_of)]


def shared_out(key, own, number, rows, number_of, top, most, skew):
    sequence = jax.random.permutation(key, number_of)
    packed, common = load_shares(number_of, rows * top, most, skew, True), load_shares(number_of, rows * top, most, skew, False)
    places = jnp.arange(number_of)

    def named(lengths, rotation):
        used = int((lengths > 0).sum())
        fixed = max(1, used // 4)
        shifted = fixed + (places - fixed + rotation * (used - fixed)) % max(1, number_of - fixed)
        return jnp.zeros((number_of,), jnp.int32).at[sequence[jnp.where(places < fixed, places, shifted)]].set(jnp.asarray(lengths, jnp.int32))

    lengths = jnp.where(number % 4 == 0, named(packed, number // 4), named(common, number - number // 4 - 1))
    mixed = jax.random.permutation(jax.random.fold_in(own, 3), number_of)
    giver, receiver = mixed[0:number_of // 2 * 2:2], mixed[1:number_of // 2 * 2:2]
    room = jnp.minimum(lengths[giver] - 1, most - lengths[receiver]) // 2
    room = jnp.where((giver == sequence[0]) | (receiver == sequence[0]) | (lengths[receiver] == 0), 0, jnp.maximum(room, 0))
    shifted = jax.random.randint(jax.random.fold_in(own, 4), (number_of // 2,), 0, 1 << 20) % (room + 1)
    lengths = lengths.at[giver].add(-shifted).at[receiver].add(shifted)
    items = jnp.searchsorted(jnp.cumsum(lengths), jnp.arange(rows * top), side="right").astype(jnp.int32)
    table = items.reshape(top, rows).T
    table = table[jax.random.permutation(jax.random.fold_in(own, 1), rows)]
    rotation = jax.random.randint(jax.random.fold_in(own, 2), (rows, 1), 0, top)
    return jnp.take_along_axis(table, (jnp.arange(top)[None, :] + rotation) % top, axis=1)


def load_shares(number_of, total, limit, skew, full):
    weights = [(1 << 20) // math.isqrt(standing ** skew) + 1 for standing in range(1, number_of + 1)]
    largest = limit if full else min(limit, max(-(-total // number_of), total * weights[0] // sum(weights)))
    least = 1 if total - largest >= number_of - 1 else 0
    holding, spare = [largest] + [least] * (number_of - 1), total - largest - least * (number_of - 1)
    while spare > 0:
        movable = [i for i in range(1, number_of) if holding[i] < largest] or [i for i in range(1, number_of) if holding[i] < limit]
        whole, remaining = sum([weights[i] for i in movable]), spare
        for i in movable:
            more = min(limit - holding[i], max(1, remaining * weights[i] // whole), spare)
            holding[i] = holding[i] + more
            spare = spare - more
    return np.array(holding)


def normal_values(key, dims, scale, limit, shards=(), held_as=jnp.bfloat16):
    loudness = level_of(key, dims, shards, -0.22, 0.18) if shards else 1.0
    array = jax.random.normal(key, dims, jnp.float32) * scale * loudness
    return jnp.minimum(jnp.maximum(array, -limit), limit).astype(held_as)


def setup_inputs(seed: int = 0) -> dict:
    key_list = jax.random.split(jax.random.key(seed), 20)
    hidden_in = normal_values(key_list[0], (TOKENS, D), 0.1, 1.5, ((0, 128),))
    attn_gain = jnp.clip(1.0 + 0.18 * jax.random.normal(key_list[1], (D,), jnp.float32), 0.1, 1.9)
    query_weight = normal_values(key_list[2], (D, HEADS * (HEAD_NOPE + ROPE)), (D // 4) ** -0.5, 0.25, ((1, 8),))
    latent_weight = normal_values(key_list[3], (D, LATENT), D ** -0.5, 0.125)
    rope_key_weight = normal_values(key_list[4], (ROPE, D), D ** -0.5, 0.125)
    latent_gain = jnp.clip(1.0 + 0.18 * jax.random.normal(key_list[5], (LATENT,), jnp.float32), 0.1, 1.9)
    kv_up_weight = normal_values(key_list[6], (LATENT, HEADS * (HEAD_NOPE + VDIM)), LATENT ** -0.5, 0.25, ((1, 8),))
    out_weight = normal_values(key_list[7], (HEADS * VDIM, D), (HEADS * VDIM // 16) ** -0.5, 0.5, ((0, 8),))
    pool_latent = jnp.clip(jax.random.uniform(key_list[8], (REQS * PAGES, PAGE, LATENT), jnp.float32, -1.6953125, 1.6953125) * level_of(key_list[8], (REQS * PAGES, PAGE, LATENT), ((0, 16),), -0.4, 0.0), -1.6953125, 1.6953125).astype(jnp.bfloat16)
    pool_rope = jnp.clip(jax.random.uniform(key_list[9], (REQS * PAGES, ROPE, PAGE), jnp.float32, -1.6953125, 1.6953125) * level_of(key_list[9], (REQS * PAGES, ROPE, PAGE), ((0, 16),), -0.4, 0.0), -1.6953125, 1.6953125).astype(jnp.bfloat16)
    page_table = jax.vmap(lambda own: jax.random.permutation(own, PAGES))(jax.random.split(key_list[10], REQS)).reshape((REQS, PAGES)).astype(jnp.int32)
    cache_len = uneven(key_list[11], REQS, REQS * MAX_CACHE // 2, MAX_CACHE, 2).astype(jnp.int32)
    post_gain = jnp.clip(1.0 + 0.18 * jax.random.normal(key_list[12], (D,), jnp.float32), 0.1, 1.9)
    router_weight = normal_values(key_list[13], (D, EXPERTS), D ** -0.5, 0.125)
    routes_keys = jax.random.split(jax.random.fold_in(key_list[14], 1), TOKENS // TOK_DEV)
    routes_turns = jax.random.permutation(jax.random.fold_in(key_list[14], 3), TOKENS // TOK_DEV)
    routes = jax.vmap(lambda own, number: shared_out(jax.random.fold_in(key_list[14], 2), own, number, TOK_DEV, EXPERTS, TOP, CAP, 2))(routes_keys, routes_turns).reshape((TOKENS, TOP))
    shared_gate_up = normal_values(key_list[15], (2, D, SHARED_FF), D ** -0.5, 0.125, ((2, 8),))
    shared_down = normal_values(key_list[16], (SHARED_FF, D), SHARED_FF ** -0.5, 0.109375, ((0, 8),))
    expert_gate_up = normal_values(key_list[17], (2 * EXPERTS, 2, D, FFE // 2), D ** -0.5, 0.125, ((0, 128),))
    expert_down = normal_values(key_list[18], (2 * EXPERTS, FFE // 2, D), (max(1, FFE // 64)) ** -0.5, 1.25, ((0, 128),))
    return dict(hidden_in=hidden_in, attn_gain=attn_gain, query_weight=query_weight, latent_weight=latent_weight, rope_key_weight=rope_key_weight, latent_gain=latent_gain, kv_up_weight=kv_up_weight, out_weight=out_weight, pool_latent=pool_latent, pool_rope=pool_rope, page_table=page_table, cache_len=cache_len, post_gain=post_gain, router_weight=router_weight, routes=routes, shared_gate_up=shared_gate_up, shared_down=shared_down, expert_gate_up=expert_gate_up, expert_down=expert_down)


EPSILON = 1e-06
THETA = 10000.0

def rms_norm(values, weights):
    widened = values.astype(jnp.float32)
    factor = lax.rsqrt(lax.optimization_barrier(jnp.mean(widened * widened, axis=-1, keepdims=True)) + EPSILON)
    return widened * factor * weights

def rounded(values):
    narrow = values.astype(jnp.bfloat16)
    return lax.optimization_barrier(narrow).astype(jnp.float32)

def rotary(values, places):
    halfway = values.shape[-1] // 2
    frequency = THETA ** (-2.0 * jnp.arange(halfway, dtype=jnp.float32) / values.shape[-1])
    angles = places[:, None] * frequency[None, :]
    cosine = jnp.cos(angles)
    sine_of = jnp.sin(angles)
    first_half = values[..., :halfway]
    second_half = values[..., halfway:]
    return jnp.concatenate([first_half * cosine - second_half * sine_of, first_half * sine_of + second_half * cosine], axis=-1)

def reference(hidden_in, attn_gain, query_weight, latent_weight, rope_key_weight, latent_gain, kv_up_weight, out_weight, pool_latent, pool_rope, page_table, cache_len, post_gain, router_weight, routes, shared_gate_up, shared_down, expert_gate_up, expert_down):
    head_width = HEAD_NOPE + ROPE
    normed = rms_norm(hidden_in, attn_gain).astype(jnp.bfloat16)
    offsets = jnp.arange(NEW_TOK, dtype=jnp.int32)
    places = (cache_len[:, None] + offsets[None, :]).reshape(TOKENS).astype(jnp.float32)
    latent_raw = jnp.dot(normed, latent_weight, preferred_element_type=jnp.float32)
    latent_new = rms_norm(latent_raw, latent_gain).astype(jnp.bfloat16)
    rope_raw = jnp.dot(normed, rope_key_weight.T, preferred_element_type=jnp.float32)
    rope_rows = rotary(rope_raw, places).astype(jnp.bfloat16)
    rope_new = rope_rows.T
    queries = jnp.dot(normed, query_weight, preferred_element_type=jnp.float32).reshape(TOKENS, HEADS, head_width)
    query_rope = rotary(jnp.swapaxes(queries[..., HEAD_NOPE:], 0, 1), places)
    query_nope = jnp.swapaxes(queries[..., :HEAD_NOPE], 0, 1)
    query_all = jnp.concatenate([query_nope, query_rope], axis=-1).astype(jnp.bfloat16)
    query_all = jnp.swapaxes(query_all.reshape(HEADS, REQS, NEW_TOK, head_width), 0, 1)
    scale_factor = float(head_width) ** (-0.5)
    key_index = jnp.arange(MAX_CACHE + NEW_TOK, dtype=jnp.int32)

    def attend(operands):
        query_rows, fresh_latent, fresh_rope, pages_latent, pages_rope, table_row, length = operands
        cached_latent = pages_latent[table_row].reshape(MAX_CACHE, LATENT)
        cached_rope = jnp.swapaxes(pages_rope[table_row], 1, 2).reshape(MAX_CACHE, ROPE)
        keys_latent = jnp.concatenate([cached_latent, fresh_latent], axis=0)
        keys_rope = jnp.concatenate([cached_rope, fresh_rope], axis=0).astype(jnp.float32)
        keys_up = jnp.dot(keys_latent, kv_up_weight, preferred_element_type=jnp.float32).astype(jnp.bfloat16)
        keys_up = keys_up.reshape(MAX_CACHE + NEW_TOK, HEADS, HEAD_NOPE + VDIM).astype(jnp.float32)
        query_wide = query_rows.astype(jnp.float32)
        scores = jnp.einsum('htc,khc->htk', query_wide[..., :HEAD_NOPE], keys_up[..., :HEAD_NOPE])
        scores = (scores + jnp.einsum('htc,kc->htk', query_wide[..., HEAD_NOPE:], keys_rope)) * scale_factor
        allowed = jnp.where(key_index[None, :] < MAX_CACHE, key_index[None, :] < length, key_index[None, :] - MAX_CACHE <= offsets[:, None])
        weights = jnp.where(allowed[None], jnp.exp(scores), 0.0)
        totals = lax.optimization_barrier(jnp.sum(weights, axis=-1))
        mixture = jnp.einsum('htk,khv->htv', rounded(weights), keys_up[..., HEAD_NOPE:])
        attended = (mixture / totals[..., None]).astype(jnp.bfloat16)
        return jnp.swapaxes(attended, 0, 1).reshape(NEW_TOK, HEADS * VDIM)
    attended_all = lax.map(attend, (query_all, latent_new.reshape(REQS, NEW_TOK, LATENT), rope_rows.reshape(REQS, NEW_TOK, ROPE), pool_latent.reshape(REQS, PAGES, PAGE, LATENT), pool_rope.reshape(REQS, PAGES, ROPE, PAGE), page_table, cache_len))
    group_heads = HEADS // N_HEAD
    out_groups = out_weight.reshape(N_HEAD, group_heads * VDIM, D).astype(jnp.float32)

    def project_out(rows_block):
        terms = jnp.einsum('tgk,gkd->gtd', rows_block.reshape(NEW_TOK, N_HEAD, group_heads * VDIM).astype(jnp.float32), out_groups)
        return lax.optimization_barrier(jnp.sum(rounded(terms), axis=0))
    attn_sum = lax.map(project_out, attended_all).reshape(TOKENS, D)
    residual = (hidden_in.astype(jnp.float32) + attn_sum).astype(jnp.bfloat16)
    post_normed = rms_norm(residual, post_gain).astype(jnp.bfloat16)
    unit_group = SHARED_FF // N_HEAD
    shared_groups = shared_down.reshape(N_HEAD, unit_group, D).astype(jnp.float32)

    def shared_block(rows_block):
        gate_part = jnp.dot(rows_block, shared_gate_up[0], preferred_element_type=jnp.float32)
        up_part = jnp.dot(rows_block, shared_gate_up[1], preferred_element_type=jnp.float32)
        inner_rows = (jax.nn.silu(gate_part) * up_part).astype(jnp.bfloat16)
        terms = jnp.einsum('tgf,gfd->gtd', inner_rows.reshape(NEW_TOK, N_HEAD, unit_group).astype(jnp.float32), shared_groups)
        return lax.optimization_barrier(jnp.sum(rounded(terms), axis=0))
    shared = lax.map(shared_block, post_normed.reshape(REQS, NEW_TOK, D)).reshape(TOKENS, D)
    logits = jnp.dot(post_normed, router_weight, preferred_element_type=jnp.float32)
    chosen_logits = jnp.take_along_axis(logits, routes, axis=1)
    raised = jnp.exp(chosen_logits)
    gate_share = raised / lax.optimization_barrier(jnp.sum(raised, axis=1, keepdims=True))
    blocks = TOKENS // TOK_DEV
    pairs = TOK_DEV * TOP
    flat_routes = routes.reshape(blocks, pairs)
    onehot = (flat_routes[..., None] == jnp.arange(EXPERTS, dtype=jnp.int32)).astype(jnp.int32)
    slot_rank = lax.optimization_barrier(jnp.sum((jnp.cumsum(onehot, axis=1, dtype=jnp.int32) - onehot) * onehot, axis=2)).astype(jnp.int32)
    block_index = jnp.broadcast_to(jnp.arange(blocks, dtype=jnp.int32)[:, None], (blocks, pairs))
    source = block_index * TOK_DEV + jnp.arange(pairs, dtype=jnp.int32)[None, :] // TOP
    slot_token = jnp.full((EXPERTS, blocks, CAP), TOKENS, dtype=jnp.int32).at[flat_routes, block_index, slot_rank].set(source)
    slot_gate = jnp.zeros((EXPERTS, blocks, CAP), dtype=jnp.float32).at[flat_routes, block_index, slot_rank].set(gate_share.reshape(blocks, pairs))
    padded_rows = jnp.concatenate([post_normed, jnp.zeros((1, D), dtype=jnp.bfloat16)], axis=0)

    def expert_step(routed_total, expert):
        index_rows = slot_token[expert].reshape(blocks * CAP)
        chosen_rows = padded_rows[index_rows]
        output_rows = jnp.zeros((blocks * CAP, D), dtype=jnp.float32)
        for which_half in range(2):
            weights_pair = expert_gate_up[2 * expert + which_half]
            gate_part = jnp.dot(chosen_rows, weights_pair[0], preferred_element_type=jnp.float32)
            up_part = jnp.dot(chosen_rows, weights_pair[1], preferred_element_type=jnp.float32)
            inner_rows = (jax.nn.silu(gate_part) * up_part).astype(jnp.bfloat16)
            output_rows = output_rows + rounded(jnp.dot(inner_rows, expert_down[2 * expert + which_half], preferred_element_type=jnp.float32))
        weighted = output_rows * slot_gate[expert].reshape(blocks * CAP)[:, None]
        return (routed_total.at[index_rows].add(weighted, mode='drop'), None)
    routed, leftover = lax.scan(expert_step, jnp.zeros((TOKENS, D), dtype=jnp.float32), jnp.arange(EXPERTS, dtype=jnp.int32))
    hidden_out = (residual.astype(jnp.float32) + shared + routed).astype(jnp.bfloat16)
    return (hidden_out, latent_new, rope_new)
```

```python
import math

import jax
import jax.numpy as jnp
from jax import lax
from jax.sharding import Mesh, PartitionSpec as P

HEAD_NOPE = 128
ROPE = 64
VDIM = 128
LATENT = 512
EXPERTS = 64
TOP = 6
HEAD_AXES = ("y", "core")
CHIP_AXES = ("req", "y")


EPSILON = 1e-06
THETA = 10000.0


def rms_norm(values, weights):
    widened = values.astype(jnp.float32)
    factor = lax.rsqrt(jnp.mean(widened * widened, axis=-1, keepdims=True) + EPSILON)
    return widened * factor * weights


def frequency_table(entries):
    return THETA ** (-2.0 * jnp.arange(entries // 2, dtype=jnp.float32) / entries)


def rotary_rows(values, places):
    halfway = values.shape[-1] // 2
    angles = places[:, None, None] * frequency_table(values.shape[-1])[None, None, :]
    cosine = jnp.cos(angles)
    sine_of = jnp.sin(angles)
    first_half = values[..., :halfway]
    second_half = values[..., halfway:]
    return jnp.concatenate(
        [first_half * cosine - second_half * sine_of, first_half * sine_of + second_half * cosine],
        axis=-1,
    )


def rotary_columns(values, places):
    halfway = values.shape[0] // 2
    angles = places[None, :] * frequency_table(values.shape[0])[:, None]
    cosine = jnp.cos(angles)
    sine_of = jnp.sin(angles)
    first_half = values[:halfway]
    second_half = values[halfway:]
    return jnp.concatenate(
        [first_half * cosine - second_half * sine_of, first_half * sine_of + second_half * cosine],
        axis=0,
    )


def body(
    hidden_in,
    attn_gain,
    query_weight,
    latent_weight,
    rope_key_weight,
    latent_gain,
    kv_up_weight,
    out_weight,
    pool_latent,
    pool_rope,
    page_table,
    cache_len,
    post_gain,
    router_weight,
    routes,
    shared_gate_up,
    shared_down,
    expert_gate_up,
    expert_down,
):
    groups = lax.axis_size("y") * lax.axis_size("core")
    member = lax.axis_index("y") * lax.axis_size("core") + lax.axis_index("core")
    own_rows = hidden_in.shape[0]
    fresh_count = own_rows * groups
    model_width = hidden_in.shape[1]
    head_width = HEAD_NOPE + ROPE
    local_heads = query_weight.shape[1] // head_width
    length = cache_len[0]
    own_start = member * own_rows
    offsets = jnp.arange(fresh_count, dtype=jnp.int32)
    places = (length + offsets).astype(jnp.float32)
    own_places = lax.dynamic_slice_in_dim(places, own_start, own_rows, 0)
    gathered = lax.all_gather(hidden_in, HEAD_AXES, axis=0, tiled=True)
    normed = rms_norm(gathered, attn_gain).astype(jnp.bfloat16)
    own_normed = lax.dynamic_slice_in_dim(normed, own_start, own_rows, 0)
    latent_raw = jnp.dot(own_normed, latent_weight, preferred_element_type=jnp.float32)
    latent_rows = rms_norm(latent_raw, latent_gain).astype(jnp.bfloat16)
    rope_raw = jnp.einsum(
        "rd,nd->rn", rope_key_weight, own_normed, preferred_element_type=jnp.float32
    )
    own_rope = rotary_columns(rope_raw, own_places).astype(jnp.bfloat16)
    fresh_latent, fresh_rope = (
        lax.all_gather(latent_rows, HEAD_AXES, axis=0, tiled=True),
        lax.all_gather(own_rope, HEAD_AXES, axis=1, tiled=True),
    )
    queries = jnp.dot(normed, query_weight, preferred_element_type=jnp.float32).reshape(
        fresh_count, local_heads, head_width
    )
    query_nope = queries[..., :HEAD_NOPE].astype(jnp.bfloat16)
    query_rope = rotary_rows(queries[..., HEAD_NOPE:], places).astype(jnp.bfloat16)
    scale_factor = float(head_width) ** (-0.5)

    def score_block(keys_latent, keys_rope):
        keys_up = jnp.dot(keys_latent, kv_up_weight, preferred_element_type=jnp.float32).astype(
            jnp.bfloat16
        )
        keys_up = keys_up.reshape(keys_latent.shape[0], local_heads, HEAD_NOPE + VDIM)
        scores = jnp.einsum(
            "thc,khc->htk", query_nope, keys_up[..., :HEAD_NOPE], preferred_element_type=jnp.float32
        )
        scores = (
            scores
            + jnp.einsum("thc,ck->htk", query_rope, keys_rope, preferred_element_type=jnp.float32)
        ) * scale_factor
        return (scores, keys_up[..., HEAD_NOPE:])

    def accumulate(running, scores, allowed, values):
        totals, mixture = running
        weights = jnp.where(allowed, jnp.exp(scores), 0.0)
        mixture = mixture + jnp.einsum(
            "htk,khv->thv", weights.astype(jnp.bfloat16), values, preferred_element_type=jnp.float32
        )
        return (totals + jnp.sum(weights, axis=-1), mixture)

    table_row = page_table[0]
    cache_rows = pool_latent.shape[0] * pool_latent.shape[1]
    cached_latent = pool_latent[table_row].reshape(cache_rows, LATENT)
    cached_rope = jnp.transpose(pool_rope[table_row], (1, 0, 2)).reshape(ROPE, cache_rows)
    stride = math.gcd(cache_rows, 512)

    def cache_step(position, running):
        first_row = position * stride
        keys_latent = lax.dynamic_slice_in_dim(cached_latent, first_row, stride, 0)
        keys_rope = lax.dynamic_slice_in_dim(cached_rope, first_row, stride, 1)
        scores, values = score_block(keys_latent, keys_rope)
        allowed = (first_row + jnp.arange(stride, dtype=jnp.int32) < length)[None, None, :]
        return accumulate(running, scores, allowed, values)

    start_state = (
        jnp.zeros((local_heads, fresh_count), jnp.float32),
        jnp.zeros((fresh_count, local_heads, VDIM), jnp.float32),
    )
    used_blocks = (length + stride - 1) // stride
    running = lax.fori_loop(0, used_blocks, cache_step, start_state)
    scores, values = score_block(fresh_latent, fresh_rope)
    allowed = (offsets[None, :] <= offsets[:, None])[None]
    totals, mixture = accumulate(running, scores, allowed, values)
    attended = (
        (mixture / jnp.transpose(totals)[..., None])
        .astype(jnp.bfloat16)
        .reshape(fresh_count, local_heads * VDIM)
    )
    rows_block = attended
    attn_sum = lax.psum_scatter(
        jnp.dot(rows_block, out_weight, preferred_element_type=jnp.float32).astype(jnp.bfloat16),
        HEAD_AXES,
        scatter_dimension=0,
        tiled=True,
    ).astype(jnp.float32)
    residual = (hidden_in.astype(jnp.float32) + attn_sum).astype(jnp.bfloat16)
    post_own = rms_norm(residual, post_gain).astype(jnp.bfloat16)
    piece = lax.all_gather(post_own, HEAD_AXES, axis=0, tiled=True)
    gate_part = jnp.dot(piece, shared_gate_up[0], preferred_element_type=jnp.float32)
    up_part = jnp.dot(piece, shared_gate_up[1], preferred_element_type=jnp.float32)
    inner_rows = (jax.nn.silu(gate_part) * up_part).astype(jnp.bfloat16)
    rows_block = inner_rows
    shared = lax.psum_scatter(
        jnp.dot(rows_block, shared_down, preferred_element_type=jnp.float32).astype(jnp.bfloat16),
        HEAD_AXES,
        scatter_dimension=0,
        tiled=True,
    ).astype(jnp.float32)
    logits = jnp.dot(post_own, router_weight, preferred_element_type=jnp.float32)
    picker = routes[:, :, None] == jnp.arange(EXPERTS, dtype=jnp.int32)[None, None, :]
    chosen_logits = jnp.sum(jnp.where(picker, logits[:, None, :], 0.0), axis=-1)
    raised = jnp.exp(chosen_logits)
    gate_share = raised / jnp.sum(raised, axis=1, keepdims=True)
    cores = lax.axis_size("core")
    capacity = max(2, own_rows * 7 // 64)
    slots = EXPERTS * capacity
    flat_routes = routes.reshape(own_rows * TOP)
    onehot = (flat_routes[:, None] == jnp.arange(EXPERTS, dtype=jnp.int32)[None, :]).astype(
        jnp.int32
    )
    slot_rank = jnp.sum((jnp.cumsum(onehot, axis=0, dtype=jnp.int32) - onehot) * onehot, axis=1)
    slot_id = (flat_routes * capacity + slot_rank).reshape(own_rows, TOP)
    picked = slot_id[:, :, None] == jnp.arange(slots, dtype=jnp.int32)[None, None, :]
    dispatch = jnp.any(picked, axis=1).astype(jnp.bfloat16)
    combine = jnp.sum(jnp.where(picked, gate_share[:, :, None], 0.0), axis=1)
    combine_hi = combine.astype(jnp.bfloat16)
    combine_lo = (combine - combine_hi.astype(jnp.float32)).astype(jnp.bfloat16)
    outgoing = jnp.einsum(
        "ts,td->sd", dispatch, post_own, preferred_element_type=jnp.float32
    ).astype(jnp.bfloat16)
    received = lax.all_to_all(
        outgoing.reshape(EXPERTS, capacity, model_width), CHIP_AXES, 0, 0, tiled=True
    )
    piece = lax.all_gather(received.reshape(slots, model_width), "core", axis=0, tiled=True)
    gate_part = jnp.dot(piece, expert_gate_up[0, 0], preferred_element_type=jnp.float32)
    up_part = jnp.dot(piece, expert_gate_up[0, 1], preferred_element_type=jnp.float32)
    inner_expert = (jax.nn.silu(gate_part) * up_part).astype(jnp.bfloat16)
    half_out = jnp.dot(inner_expert, expert_down[0], preferred_element_type=jnp.float32).astype(
        jnp.bfloat16
    )
    halves = lax.all_to_all(
        half_out.reshape(cores, slots, model_width), "core", 0, 0, tiled=True
    ).astype(jnp.float32)
    summed = jnp.sum(halves, axis=0).astype(jnp.bfloat16)
    returned = lax.all_to_all(
        summed.reshape(EXPERTS, capacity, model_width), CHIP_AXES, 0, 0, tiled=True
    ).reshape(slots, model_width)
    routed = jnp.dot(combine_hi, returned, preferred_element_type=jnp.float32) + jnp.dot(
        combine_lo, returned, preferred_element_type=jnp.float32
    )
    hidden_out = (residual.astype(jnp.float32) + shared + routed).astype(jnp.bfloat16)
    return (hidden_out, latent_rows, own_rope)


def solution(mesh):
    chip_mesh = Mesh(
        mesh.devices.reshape(mesh.devices.shape[0], -1, 2), ("req",) + HEAD_AXES
    )
    placed = (
        P(("req",) + HEAD_AXES, None),
        P(),
        P(None, HEAD_AXES),
        P(),
        P(),
        P(),
        P(None, HEAD_AXES),
        P(HEAD_AXES, None),
        P("req", None, None),
        P("req", None, None),
        P("req", None),
        P("req"),
        P(),
        P(),
        P(("req",) + HEAD_AXES, None),
        P(None, None, HEAD_AXES),
        P(HEAD_AXES, None),
        P(("req",) + HEAD_AXES, None, None, None),
        P(("req",) + HEAD_AXES, None, None),
    )
    return jax.shard_map(
        body,
        mesh=chip_mesh,
        in_specs=placed,
        out_specs=(P(("req",) + HEAD_AXES, None), P(("req",) + HEAD_AXES, None), P(None, ("req",) + HEAD_AXES)),
        check_vma=False,
    )
```

```python
import math

import jax
import jax.numpy as jnp
from jax import lax
from jax.sharding import Mesh, PartitionSpec as P

HEAD_NOPE = 128
ROPE = 64
VDIM = 128
LATENT = 512
EXPERTS = 64
TOP = 6
HEAD_AXES = ("y", "core")
CHIP_AXES = ("req", "y")


EPSILON = 1e-06
THETA = 10000.0


def rms_norm(values, weights):
    widened = values.astype(jnp.float32)
    factor = lax.rsqrt(jnp.mean(widened * widened, axis=-1, keepdims=True) + EPSILON)
    return widened * factor * weights


def frequency_table(entries):
    return THETA ** (-2.0 * jnp.arange(entries // 2, dtype=jnp.float32) / entries)


def rotary_rows(values, places):
    halfway = values.shape[-1] // 2
    angles = places[:, None, None] * frequency_table(values.shape[-1])[None, None, :]
    cosine = jnp.cos(angles)
    sine_of = jnp.sin(angles)
    first_half = values[..., :halfway]
    second_half = values[..., halfway:]
    return jnp.concatenate(
        [first_half * cosine - second_half * sine_of, first_half * sine_of + second_half * cosine],
        axis=-1,
    )


def rotary_columns(values, places):
    halfway = values.shape[0] // 2
    angles = places[None, :] * frequency_table(values.shape[0])[:, None]
    cosine = jnp.cos(angles)
    sine_of = jnp.sin(angles)
    first_half = values[:halfway]
    second_half = values[halfway:]
    return jnp.concatenate(
        [first_half * cosine - second_half * sine_of, first_half * sine_of + second_half * cosine],
        axis=0,
    )


def body(
    hidden_in,
    attn_gain,
    query_weight,
    latent_weight,
    rope_key_weight,
    latent_gain,
    kv_up_weight,
    out_weight,
    pool_latent,
    pool_rope,
    page_table,
    cache_len,
    post_gain,
    router_weight,
    routes,
    shared_gate_up,
    shared_down,
    expert_gate_up,
    expert_down,
):
    groups = lax.axis_size("y") * lax.axis_size("core")
    member = lax.axis_index("y") * lax.axis_size("core") + lax.axis_index("core")
    own_rows = hidden_in.shape[0]
    fresh_count = own_rows * groups
    model_width = hidden_in.shape[1]
    head_width = HEAD_NOPE + ROPE
    local_heads = query_weight.shape[1] // head_width
    length = cache_len[0]
    own_start = member * own_rows
    offsets = jnp.arange(fresh_count, dtype=jnp.int32)
    places = (length + offsets).astype(jnp.float32)
    own_places = lax.dynamic_slice_in_dim(places, own_start, own_rows, 0)
    own_normed = rms_norm(hidden_in, attn_gain).astype(jnp.bfloat16)
    latent_raw = jnp.dot(own_normed, latent_weight, preferred_element_type=jnp.float32)
    latent_rows = rms_norm(latent_raw, latent_gain).astype(jnp.bfloat16)
    rope_raw = jnp.einsum(
        "rd,nd->rn", rope_key_weight, own_normed, preferred_element_type=jnp.float32
    )
    own_rope = rotary_columns(rope_raw, own_places).astype(jnp.bfloat16)
    fresh_latent, fresh_rope = (
        lax.all_gather(latent_rows, HEAD_AXES, axis=0, tiled=True),
        lax.all_gather(own_rope, HEAD_AXES, axis=1, tiled=True),
    )
    scale_factor = float(head_width) ** (-0.5)
    table_row = page_table[0]
    cache_rows = pool_latent.shape[0] * pool_latent.shape[1]
    cached_latent = pool_latent[table_row].reshape(cache_rows, LATENT)
    cached_rope = jnp.transpose(pool_rope[table_row], (1, 0, 2)).reshape(ROPE, cache_rows)
    stride = math.gcd(cache_rows, 512)

    def keys_of(keys_latent):
        keys_up = jnp.dot(keys_latent, kv_up_weight, preferred_element_type=jnp.float32).astype(
            jnp.bfloat16
        )
        return keys_up.reshape(keys_latent.shape[0], local_heads, HEAD_NOPE + VDIM)

    cached_up = keys_of(cached_latent)
    fresh_up = keys_of(fresh_latent)

    def accumulate(running, scores, allowed, values):
        totals, mixture = running
        weights = jnp.where(allowed, jnp.exp(scores), 0.0)
        mixture = mixture + jnp.einsum(
            "htk,khv->thv", weights.astype(jnp.bfloat16), values, preferred_element_type=jnp.float32
        )
        return (totals + jnp.sum(weights, axis=-1), mixture)

    def attend(normed_rows, query_offsets):
        count = normed_rows.shape[0]
        query_places = (length + query_offsets).astype(jnp.float32)
        queries = jnp.dot(normed_rows, query_weight, preferred_element_type=jnp.float32).reshape(
            count, local_heads, head_width
        )
        query_nope = queries[..., :HEAD_NOPE].astype(jnp.bfloat16)
        query_rope = rotary_rows(queries[..., HEAD_NOPE:], query_places).astype(jnp.bfloat16)

        def score_block(keys_up, keys_rope):
            scores = jnp.einsum(
                "thc,khc->htk", query_nope, keys_up[..., :HEAD_NOPE],
                preferred_element_type=jnp.float32,
            )
            scores = (
                scores
                + jnp.einsum(
                    "thc,ck->htk", query_rope, keys_rope, preferred_element_type=jnp.float32
                )
            ) * scale_factor
            return (scores, keys_up[..., HEAD_NOPE:])

        def cache_step(position, running):
            first_row = position * stride
            keys_up = lax.dynamic_slice_in_dim(cached_up, first_row, stride, 0)
            keys_rope = lax.dynamic_slice_in_dim(cached_rope, first_row, stride, 1)
            scores, values = score_block(keys_up, keys_rope)
            allowed = (first_row + jnp.arange(stride, dtype=jnp.int32) < length)[None, None, :]
            return accumulate(running, scores, allowed, values)

        start_state = (
            jnp.zeros((local_heads, count), jnp.float32),
            jnp.zeros((count, local_heads, VDIM), jnp.float32),
        )
        used_blocks = (length + stride - 1) // stride
        running = lax.fori_loop(0, used_blocks, cache_step, start_state)
        scores, values = score_block(fresh_up, fresh_rope)
        allowed = (offsets[None, :] <= query_offsets[:, None])[None]
        totals, mixture = accumulate(running, scores, allowed, values)
        attended = (
            (mixture / jnp.transpose(totals)[..., None])
            .astype(jnp.bfloat16)
            .reshape(count, local_heads * VDIM)
        )
        return lax.psum_scatter(
            jnp.dot(attended, out_weight, preferred_element_type=jnp.float32).astype(jnp.bfloat16),
            HEAD_AXES,
            scatter_dimension=0,
            tiled=True,
        ).astype(jnp.float32)

    chunk_count = 2
    chunk_rows = own_rows // chunk_count
    sums = []
    for chunk in range(chunk_count):
        rows = lax.all_gather(
            own_normed[chunk * chunk_rows:(chunk + 1) * chunk_rows], HEAD_AXES, axis=0, tiled=True
        )
        query_offsets = (
            jnp.arange(groups, dtype=jnp.int32)[:, None] * own_rows
            + chunk * chunk_rows
            + jnp.arange(chunk_rows, dtype=jnp.int32)[None, :]
        ).reshape(groups * chunk_rows)
        sums.append(attend(rows, query_offsets))
    attn_sum = jnp.concatenate(sums, axis=0)
    residual = (hidden_in.astype(jnp.float32) + attn_sum).astype(jnp.bfloat16)
    post_own = rms_norm(residual, post_gain).astype(jnp.bfloat16)
    piece = lax.all_gather(post_own, HEAD_AXES, axis=0, tiled=True)
    gate_part = jnp.dot(piece, shared_gate_up[0], preferred_element_type=jnp.float32)
    up_part = jnp.dot(piece, shared_gate_up[1], preferred_element_type=jnp.float32)
    inner_rows = (jax.nn.silu(gate_part) * up_part).astype(jnp.bfloat16)
    rows_block = inner_rows
    shared = lax.psum_scatter(
        jnp.dot(rows_block, shared_down, preferred_element_type=jnp.float32).astype(jnp.bfloat16),
        HEAD_AXES,
        scatter_dimension=0,
        tiled=True,
    ).astype(jnp.float32)
    logits = jnp.dot(post_own, router_weight, preferred_element_type=jnp.float32)
    picker = routes[:, :, None] == jnp.arange(EXPERTS, dtype=jnp.int32)[None, None, :]
    chosen_logits = jnp.sum(jnp.where(picker, logits[:, None, :], 0.0), axis=-1)
    raised = jnp.exp(chosen_logits)
    gate_share = raised / jnp.sum(raised, axis=1, keepdims=True)
    cores = lax.axis_size("core")
    capacity = max(2, own_rows * 7 // 64)
    slots = EXPERTS * capacity
    flat_routes = routes.reshape(own_rows * TOP)
    onehot = (flat_routes[:, None] == jnp.arange(EXPERTS, dtype=jnp.int32)[None, :]).astype(
        jnp.int32
    )
    slot_rank = jnp.sum((jnp.cumsum(onehot, axis=0, dtype=jnp.int32) - onehot) * onehot, axis=1)
    slot_id = (flat_routes * capacity + slot_rank).reshape(own_rows, TOP)
    picked = slot_id[:, :, None] == jnp.arange(slots, dtype=jnp.int32)[None, None, :]
    dispatch = jnp.any(picked, axis=1).astype(jnp.bfloat16)
    combine = jnp.sum(jnp.where(picked, gate_share[:, :, None], 0.0), axis=1)
    combine_hi = combine.astype(jnp.bfloat16)
    combine_lo = (combine - combine_hi.astype(jnp.float32)).astype(jnp.bfloat16)
    outgoing = jnp.einsum(
        "ts,td->sd", dispatch, post_own, preferred_element_type=jnp.float32
    ).astype(jnp.bfloat16)
    received = lax.all_to_all(
        outgoing.reshape(EXPERTS, capacity, model_width), CHIP_AXES, 0, 0, tiled=True
    )
    piece = lax.all_gather(received.reshape(slots, model_width), "core", axis=0, tiled=True)
    gate_part = jnp.dot(piece, expert_gate_up[0, 0], preferred_element_type=jnp.float32)
    up_part = jnp.dot(piece, expert_gate_up[0, 1], preferred_element_type=jnp.float32)
    inner_expert = (jax.nn.silu(gate_part) * up_part).astype(jnp.bfloat16)
    half_out = jnp.dot(inner_expert, expert_down[0], preferred_element_type=jnp.float32).astype(
        jnp.bfloat16
    )
    halves = lax.all_to_all(
        half_out.reshape(cores, slots, model_width), "core", 0, 0, tiled=True
    ).astype(jnp.float32)
    summed = jnp.sum(halves, axis=0).astype(jnp.bfloat16)
    returned = lax.all_to_all(
        summed.reshape(EXPERTS, capacity, model_width), CHIP_AXES, 0, 0, tiled=True
    ).reshape(slots, model_width)
    routed = jnp.dot(combine_hi, returned, preferred_element_type=jnp.float32) + jnp.dot(
        combine_lo, returned, preferred_element_type=jnp.float32
    )
    hidden_out = (residual.astype(jnp.float32) + shared + routed).astype(jnp.bfloat16)
    return (hidden_out, latent_rows, own_rope)


def solution(mesh):
    chip_mesh = Mesh(
        mesh.devices.reshape(mesh.devices.shape[0], -1, 2), ("req",) + HEAD_AXES
    )
    placed = (
        P(("req",) + HEAD_AXES, None),
        P(),
        P(None, HEAD_AXES),
        P(),
        P(),
        P(),
        P(None, HEAD_AXES),
        P(HEAD_AXES, None),
        P("req", None, None),
        P("req", None, None),
        P("req", None),
        P("req"),
        P(),
        P(),
        P(("req",) + HEAD_AXES, None),
        P(None, None, HEAD_AXES),
        P(HEAD_AXES, None),
        P(("req",) + HEAD_AXES, None, None, None),
        P(("req",) + HEAD_AXES, None, None),
    )
    return jax.shard_map(
        body,
        mesh=chip_mesh,
        in_specs=placed,
        out_specs=(P(("req",) + HEAD_AXES, None), P(("req",) + HEAD_AXES, None), P(None, ("req",) + HEAD_AXES)),
        check_vma=False,
    )
```

```python
import math

import jax
import jax.numpy as jnp
from jax import lax
from jax.sharding import Mesh, PartitionSpec as P


HEAD_NOPE = 128
ROPE = 64
VDIM = 128
LATENT = 512
EXPERTS = 64
TOP = 6
HEAD_AXES = ("y", "core")
CHIP_AXES = ("req", "y")


EPSILON = 1e-06
THETA = 10000.0


def rms_norm(values, weights):
    widened = values.astype(jnp.float32)
    factor = lax.rsqrt(jnp.mean(widened * widened, axis=-1, keepdims=True) + EPSILON)
    return widened * factor * weights


def frequency_table(entries):
    return THETA ** (-2.0 * jnp.arange(entries // 2, dtype=jnp.float32) / entries)


def rotary_rows(values, places):
    halfway = values.shape[-1] // 2
    angles = places[:, None, None] * frequency_table(values.shape[-1])[None, None, :]
    cosine = jnp.cos(angles)
    sine_of = jnp.sin(angles)
    first_half = values[..., :halfway]
    second_half = values[..., halfway:]
    return jnp.concatenate(
        [first_half * cosine - second_half * sine_of, first_half * sine_of + second_half * cosine],
        axis=-1,
    )


def rotary_columns(values, places):
    halfway = values.shape[0] // 2
    angles = places[None, :] * frequency_table(values.shape[0])[:, None]
    cosine = jnp.cos(angles)
    sine_of = jnp.sin(angles)
    first_half = values[:halfway]
    second_half = values[halfway:]
    return jnp.concatenate(
        [first_half * cosine - second_half * sine_of, first_half * sine_of + second_half * cosine],
        axis=0,
    )


def body(
    hidden_in,
    attn_gain,
    query_weight,
    latent_weight,
    rope_key_weight,
    latent_gain,
    kv_up_weight,
    out_weight,
    pool_latent,
    pool_rope,
    page_table,
    cache_len,
    post_gain,
    router_weight,
    routes,
    shared_gate_up,
    shared_down,
    expert_gate_up,
    expert_down,
):
    swap = [(0, 1), (1, 0)]
    mate_gate_up = lax.ppermute(expert_gate_up, "core", swap)
    mate_down = lax.ppermute(expert_down, "core", swap)
    groups = lax.axis_size("y") * lax.axis_size("core")
    member = lax.axis_index("y") * lax.axis_size("core") + lax.axis_index("core")
    own_rows = hidden_in.shape[0]
    fresh_count = own_rows * groups
    model_width = hidden_in.shape[1]
    head_width = HEAD_NOPE + ROPE
    local_heads = query_weight.shape[1] // head_width
    length = cache_len[0]
    own_start = member * own_rows
    offsets = jnp.arange(fresh_count, dtype=jnp.int32)
    places = (length + offsets).astype(jnp.float32)
    own_places = lax.dynamic_slice_in_dim(places, own_start, own_rows, 0)
    own_normed = rms_norm(hidden_in, attn_gain).astype(jnp.bfloat16)
    latent_raw = jnp.dot(own_normed, latent_weight, preferred_element_type=jnp.float32)
    latent_rows = rms_norm(latent_raw, latent_gain).astype(jnp.bfloat16)
    rope_raw = jnp.einsum(
        "rd,nd->rn", rope_key_weight, own_normed, preferred_element_type=jnp.float32
    )
    own_rope = rotary_columns(rope_raw, own_places).astype(jnp.bfloat16)
    lane_pad = -ROPE % 128
    packed = jnp.concatenate(
        [
            own_normed,
            latent_rows,
            jnp.transpose(own_rope),
            jnp.zeros((own_rows, lane_pad), jnp.bfloat16),
        ],
        axis=1,
    )
    gathered = lax.all_gather(packed, HEAD_AXES, axis=0, tiled=True)
    normed = gathered[:, :model_width]
    fresh_latent = gathered[:, model_width:model_width + LATENT]
    fresh_rope = jnp.transpose(gathered[:, model_width + LATENT:model_width + LATENT + ROPE])
    queries = jnp.dot(normed, query_weight, preferred_element_type=jnp.float32).reshape(
        fresh_count, local_heads, head_width
    )
    query_nope = queries[..., :HEAD_NOPE].astype(jnp.bfloat16)
    query_rope = rotary_rows(queries[..., HEAD_NOPE:], places).astype(jnp.bfloat16)
    scale_factor = float(head_width) ** (-0.5)

    def score_block(keys_latent, keys_rope):
        keys_up = jnp.dot(keys_latent, kv_up_weight, preferred_element_type=jnp.float32).astype(
            jnp.bfloat16
        )
        keys_up = keys_up.reshape(keys_latent.shape[0], local_heads, HEAD_NOPE + VDIM)
        scores = jnp.einsum(
            "thc,khc->htk", query_nope, keys_up[..., :HEAD_NOPE], preferred_element_type=jnp.float32
        )
        scores = (
            scores
            + jnp.einsum("thc,ck->htk", query_rope, keys_rope, preferred_element_type=jnp.float32)
        ) * scale_factor
        return (scores, keys_up[..., HEAD_NOPE:])

    def accumulate(running, scores, allowed, values):
        totals, mixture = running
        weights = jnp.where(allowed, jnp.exp(scores), 0.0)
        mixture = mixture + jnp.einsum(
            "htk,khv->thv", weights.astype(jnp.bfloat16), values, preferred_element_type=jnp.float32
        )
        return (totals + jnp.sum(weights, axis=-1), mixture)

    table_row = page_table[0]
    cache_rows = pool_latent.shape[0] * pool_latent.shape[1]
    cached_latent = pool_latent[table_row].reshape(cache_rows, LATENT)
    cached_rope = jnp.transpose(pool_rope[table_row], (1, 0, 2)).reshape(ROPE, cache_rows)
    stride = math.gcd(cache_rows, 512)

    def cache_step(position, running):
        first_row = position * stride
        keys_latent = lax.dynamic_slice_in_dim(cached_latent, first_row, stride, 0)
        keys_rope = lax.dynamic_slice_in_dim(cached_rope, first_row, stride, 1)
        scores, values = score_block(keys_latent, keys_rope)
        allowed = (first_row + jnp.arange(stride, dtype=jnp.int32) < length)[None, None, :]
        return accumulate(running, scores, allowed, values)

    start_state = (
        jnp.zeros((local_heads, fresh_count), jnp.float32),
        jnp.zeros((fresh_count, local_heads, VDIM), jnp.float32),
    )
    used_blocks = (length + stride - 1) // stride
    running = lax.fori_loop(0, used_blocks, cache_step, start_state)
    scores, values = score_block(fresh_latent, fresh_rope)
    allowed = (offsets[None, :] <= offsets[:, None])[None]
    totals, mixture = accumulate(running, scores, allowed, values)
    attended = (
        (mixture / jnp.transpose(totals)[..., None])
        .astype(jnp.bfloat16)
        .reshape(fresh_count, local_heads * VDIM)
    )
    rows_block = attended
    attn_sum = lax.psum_scatter(
        jnp.dot(rows_block, out_weight, preferred_element_type=jnp.float32).astype(jnp.bfloat16),
        HEAD_AXES,
        scatter_dimension=0,
        tiled=True,
    ).astype(jnp.float32)
    residual = (hidden_in.astype(jnp.float32) + attn_sum).astype(jnp.bfloat16)
    post_own = rms_norm(residual, post_gain).astype(jnp.bfloat16)
    piece = lax.all_gather(post_own, HEAD_AXES, axis=0, tiled=True)
    gate_part = jnp.dot(piece, shared_gate_up[0], preferred_element_type=jnp.float32)
    up_part = jnp.dot(piece, shared_gate_up[1], preferred_element_type=jnp.float32)
    inner_rows = (jax.nn.silu(gate_part) * up_part).astype(jnp.bfloat16)
    rows_block = inner_rows
    shared = lax.psum_scatter(
        jnp.dot(rows_block, shared_down, preferred_element_type=jnp.float32).astype(jnp.bfloat16),
        HEAD_AXES,
        scatter_dimension=0,
        tiled=True,
    ).astype(jnp.float32)
    logits = jnp.dot(post_own, router_weight, preferred_element_type=jnp.float32)
    picker = routes[:, :, None] == jnp.arange(EXPERTS, dtype=jnp.int32)[None, None, :]
    chosen_logits = jnp.sum(jnp.where(picker, logits[:, None, :], 0.0), axis=-1)
    raised = jnp.exp(chosen_logits)
    gate_share = raised / jnp.sum(raised, axis=1, keepdims=True)
    capacity = max(2, own_rows * 7 // 64)
    slots = EXPERTS * capacity
    flat_routes = routes.reshape(own_rows * TOP)
    onehot = (flat_routes[:, None] == jnp.arange(EXPERTS, dtype=jnp.int32)[None, :]).astype(
        jnp.int32
    )
    slot_rank = jnp.sum((jnp.cumsum(onehot, axis=0, dtype=jnp.int32) - onehot) * onehot, axis=1)
    slot_id = (flat_routes * capacity + slot_rank).reshape(own_rows, TOP)
    picked = slot_id[:, :, None] == jnp.arange(slots, dtype=jnp.int32)[None, None, :]
    dispatch = jnp.any(picked, axis=1).astype(jnp.bfloat16)
    combine = jnp.sum(jnp.where(picked, gate_share[:, :, None], 0.0), axis=1)
    combine_hi = combine.astype(jnp.bfloat16)
    combine_lo = (combine - combine_hi.astype(jnp.float32)).astype(jnp.bfloat16)
    outgoing = jnp.einsum(
        "ts,td->sd", dispatch, post_own, preferred_element_type=jnp.float32
    ).astype(jnp.bfloat16)
    received = lax.all_to_all(
        outgoing.reshape(EXPERTS, capacity, model_width), CHIP_AXES, 0, 0, tiled=True
    )
    piece = received.reshape(slots, model_width)

    def expert_half(gate_up, down):
        gate_part = jnp.dot(piece, gate_up[0], preferred_element_type=jnp.float32)
        up_part = jnp.dot(piece, gate_up[1], preferred_element_type=jnp.float32)
        inner_expert = (jax.nn.silu(gate_part) * up_part).astype(jnp.bfloat16)
        return jnp.dot(inner_expert, down, preferred_element_type=jnp.float32).astype(
            jnp.bfloat16
        )

    summed = (
        expert_half(expert_gate_up[0], expert_down[0]).astype(jnp.float32)
        + expert_half(mate_gate_up[0], mate_down[0]).astype(jnp.float32)
    ).astype(jnp.bfloat16)
    returned = lax.all_to_all(
        summed.reshape(EXPERTS, capacity, model_width), CHIP_AXES, 0, 0, tiled=True
    ).reshape(slots, model_width)
    routed = jnp.dot(combine_hi, returned, preferred_element_type=jnp.float32) + jnp.dot(
        combine_lo, returned, preferred_element_type=jnp.float32
    )
    hidden_out = (residual.astype(jnp.float32) + shared + routed).astype(jnp.bfloat16)
    return (hidden_out, latent_rows, own_rope)


def solution(mesh):
    chip_mesh = Mesh(
        mesh.devices.reshape(mesh.devices.shape[0], -1, 2), ("req",) + HEAD_AXES
    )
    placed = (
        P(("req",) + HEAD_AXES, None),
        P(),
        P(None, HEAD_AXES),
        P(),
        P(),
        P(),
        P(None, HEAD_AXES),
        P(HEAD_AXES, None),
        P("req", None, None),
        P("req", None, None),
        P("req", None),
        P("req"),
        P(),
        P(),
        P(("req",) + HEAD_AXES, None),
        P(None, None, HEAD_AXES),
        P(HEAD_AXES, None),
        P(("req",) + HEAD_AXES, None, None, None),
        P(("req",) + HEAD_AXES, None, None),
    )
    return jax.shard_map(
        body,
        mesh=chip_mesh,
        in_specs=placed,
        out_specs=(P(("req",) + HEAD_AXES, None), P(("req",) + HEAD_AXES, None), P(None, ("req",) + HEAD_AXES)),
        check_vma=False,
    )
```

```python
import math

import jax
import jax.numpy as jnp
from jax import lax
from jax.sharding import Mesh, PartitionSpec as P


HEAD_NOPE = 128
ROPE = 64
VDIM = 128
LATENT = 512
EXPERTS = 64
TOP = 6
HEAD_AXES = ("y", "core")
CHIP_AXES = ("req", "y")


EPSILON = 1e-06
THETA = 10000.0


def rms_norm(values, weights):
    widened = values.astype(jnp.float32)
    factor = lax.rsqrt(jnp.mean(widened * widened, axis=-1, keepdims=True) + EPSILON)
    return widened * factor * weights


def frequency_table(entries):
    return THETA ** (-2.0 * jnp.arange(entries // 2, dtype=jnp.float32) / entries)


def rotary_rows(values, places):
    halfway = values.shape[-1] // 2
    angles = places[:, None, None] * frequency_table(values.shape[-1])[None, None, :]
    cosine = jnp.cos(angles)
    sine_of = jnp.sin(angles)
    first_half = values[..., :halfway]
    second_half = values[..., halfway:]
    return jnp.concatenate(
        [first_half * cosine - second_half * sine_of, first_half * sine_of + second_half * cosine],
        axis=-1,
    )


def rotary_columns(values, places):
    halfway = values.shape[0] // 2
    angles = places[None, :] * frequency_table(values.shape[0])[:, None]
    cosine = jnp.cos(angles)
    sine_of = jnp.sin(angles)
    first_half = values[:halfway]
    second_half = values[halfway:]
    return jnp.concatenate(
        [first_half * cosine - second_half * sine_of, first_half * sine_of + second_half * cosine],
        axis=0,
    )


def body(
    hidden_in,
    attn_gain,
    query_weight,
    latent_weight,
    rope_key_weight,
    latent_gain,
    kv_up_weight,
    out_weight,
    pool_latent,
    pool_rope,
    page_table,
    cache_len,
    post_gain,
    router_weight,
    routes,
    shared_gate_up,
    shared_down,
    expert_gate_up,
    expert_down,
):
    swap = [(0, 1), (1, 0)]
    mate_gate_up = lax.ppermute(expert_gate_up, "core", swap)
    mate_down = lax.ppermute(expert_down, "core", swap)
    groups = lax.axis_size("y") * lax.axis_size("core")
    member = lax.axis_index("y") * lax.axis_size("core") + lax.axis_index("core")
    own_rows = hidden_in.shape[0]
    fresh_count = own_rows * groups
    model_width = hidden_in.shape[1]
    head_width = HEAD_NOPE + ROPE
    local_heads = query_weight.shape[1] // head_width
    length = cache_len[0]
    own_start = member * own_rows
    offsets = jnp.arange(fresh_count, dtype=jnp.int32)
    places = (length + offsets).astype(jnp.float32)
    own_places = lax.dynamic_slice_in_dim(places, own_start, own_rows, 0)
    gathered = lax.all_gather(hidden_in, HEAD_AXES, axis=0, tiled=True)
    normed = rms_norm(gathered, attn_gain).astype(jnp.bfloat16)
    own_normed = lax.dynamic_slice_in_dim(normed, own_start, own_rows, 0)
    latent_raw = jnp.dot(own_normed, latent_weight, preferred_element_type=jnp.float32)
    latent_rows = rms_norm(latent_raw, latent_gain).astype(jnp.bfloat16)
    rope_raw = jnp.einsum(
        "rd,nd->rn", rope_key_weight, own_normed, preferred_element_type=jnp.float32
    )
    own_rope = rotary_columns(rope_raw, own_places).astype(jnp.bfloat16)
    fresh_latent, fresh_rope = (
        lax.all_gather(latent_rows, HEAD_AXES, axis=0, tiled=True),
        lax.all_gather(own_rope, HEAD_AXES, axis=1, tiled=True),
    )
    queries = jnp.dot(normed, query_weight, preferred_element_type=jnp.float32).reshape(
        fresh_count, local_heads, head_width
    )
    query_nope = queries[..., :HEAD_NOPE].astype(jnp.bfloat16)
    query_rope = rotary_rows(queries[..., HEAD_NOPE:], places).astype(jnp.bfloat16)
    scale_factor = float(head_width) ** (-0.5)

    def score_block(keys_latent, keys_rope):
        keys_up = jnp.dot(keys_latent, kv_up_weight, preferred_element_type=jnp.float32).astype(
            jnp.bfloat16
        )
        keys_up = keys_up.reshape(keys_latent.shape[0], local_heads, HEAD_NOPE + VDIM)
        scores = jnp.einsum(
            "thc,khc->htk", query_nope, keys_up[..., :HEAD_NOPE], preferred_element_type=jnp.float32
        )
        scores = (
            scores
            + jnp.einsum("thc,ck->htk", query_rope, keys_rope, preferred_element_type=jnp.float32)
        ) * scale_factor
        return (scores, keys_up[..., HEAD_NOPE:])

    def accumulate(running, scores, allowed, values):
        totals, mixture = running
        weights = jnp.where(allowed, jnp.exp(scores), 0.0)
        mixture = mixture + jnp.einsum(
            "htk,khv->thv", weights.astype(jnp.bfloat16), values, preferred_element_type=jnp.float32
        )
        return (totals + jnp.sum(weights, axis=-1), mixture)

    table_row = page_table[0]
    cache_rows = pool_latent.shape[0] * pool_latent.shape[1]
    cached_latent = pool_latent[table_row].reshape(cache_rows, LATENT)
    cached_rope = jnp.transpose(pool_rope[table_row], (1, 0, 2)).reshape(ROPE, cache_rows)
    stride = math.gcd(cache_rows, 512)

    def cache_step(position, running):
        first_row = position * stride
        keys_latent = lax.dynamic_slice_in_dim(cached_latent, first_row, stride, 0)
        keys_rope = lax.dynamic_slice_in_dim(cached_rope, first_row, stride, 1)
        scores, values = score_block(keys_latent, keys_rope)
        allowed = (first_row + jnp.arange(stride, dtype=jnp.int32) < length)[None, None, :]
        return accumulate(running, scores, allowed, values)

    start_state = (
        jnp.zeros((local_heads, fresh_count), jnp.float32),
        jnp.zeros((fresh_count, local_heads, VDIM), jnp.float32),
    )
    used_blocks = (length + stride - 1) // stride
    running = lax.fori_loop(0, used_blocks, cache_step, start_state)
    scores, values = score_block(fresh_latent, fresh_rope)
    allowed = (offsets[None, :] <= offsets[:, None])[None]
    totals, mixture = accumulate(running, scores, allowed, values)
    attended = (
        (mixture / jnp.transpose(totals)[..., None])
        .astype(jnp.bfloat16)
        .reshape(fresh_count, local_heads * VDIM)
    )
    rows_block = attended
    attn_sum = lax.psum_scatter(
        jnp.dot(rows_block, out_weight, preferred_element_type=jnp.float32).astype(jnp.bfloat16),
        HEAD_AXES,
        scatter_dimension=0,
        tiled=True,
    ).astype(jnp.float32)
    residual = (hidden_in.astype(jnp.float32) + attn_sum).astype(jnp.bfloat16)
    post_own = rms_norm(residual, post_gain).astype(jnp.bfloat16)
    piece = lax.all_gather(post_own, HEAD_AXES, axis=0, tiled=True)
    gate_part = jnp.dot(piece, shared_gate_up[0], preferred_element_type=jnp.float32)
    up_part = jnp.dot(piece, shared_gate_up[1], preferred_element_type=jnp.float32)
    inner_rows = (jax.nn.silu(gate_part) * up_part).astype(jnp.bfloat16)
    rows_block = inner_rows
    shared = lax.psum_scatter(
        jnp.dot(rows_block, shared_down, preferred_element_type=jnp.float32).astype(jnp.bfloat16),
        HEAD_AXES,
        scatter_dimension=0,
        tiled=True,
    ).astype(jnp.float32)
    logits = jnp.dot(post_own, router_weight, preferred_element_type=jnp.float32)
    picker = routes[:, :, None] == jnp.arange(EXPERTS, dtype=jnp.int32)[None, None, :]
    chosen_logits = jnp.sum(jnp.where(picker, logits[:, None, :], 0.0), axis=-1)
    raised = jnp.exp(chosen_logits)
    gate_share = raised / jnp.sum(raised, axis=1, keepdims=True)
    capacity = -(-max(2, own_rows * 7 // 64) // 16) * 16
    slots = EXPERTS * capacity
    flat_routes = routes.reshape(own_rows * TOP)
    onehot = (flat_routes[:, None] == jnp.arange(EXPERTS, dtype=jnp.int32)[None, :]).astype(
        jnp.int32
    )
    slot_rank = jnp.sum((jnp.cumsum(onehot, axis=0, dtype=jnp.int32) - onehot) * onehot, axis=1)
    slot_id = (flat_routes * capacity + slot_rank).reshape(own_rows, TOP)
    picked = slot_id[:, :, None] == jnp.arange(slots, dtype=jnp.int32)[None, None, :]
    dispatch = jnp.any(picked, axis=1).astype(jnp.bfloat16)
    combine = jnp.sum(jnp.where(picked, gate_share[:, :, None], 0.0), axis=1)
    combine_hi = combine.astype(jnp.bfloat16)
    combine_lo = (combine - combine_hi.astype(jnp.float32)).astype(jnp.bfloat16)
    outgoing = jnp.einsum(
        "ts,td->sd", dispatch, post_own, preferred_element_type=jnp.float32
    ).astype(jnp.bfloat16)
    received = lax.all_to_all(
        outgoing.reshape(EXPERTS, capacity, model_width), CHIP_AXES, 0, 0, tiled=True
    )
    piece = received.reshape(slots, model_width)

    def expert_half(gate_up, down):
        gate_part = jnp.dot(piece, gate_up[0], preferred_element_type=jnp.float32)
        up_part = jnp.dot(piece, gate_up[1], preferred_element_type=jnp.float32)
        inner_expert = (jax.nn.silu(gate_part) * up_part).astype(jnp.bfloat16)
        return jnp.dot(inner_expert, down, preferred_element_type=jnp.float32).astype(
            jnp.bfloat16
        )

    summed = (
        expert_half(expert_gate_up[0], expert_down[0]).astype(jnp.float32)
        + expert_half(mate_gate_up[0], mate_down[0]).astype(jnp.float32)
    ).astype(jnp.bfloat16)
    returned = lax.all_to_all(
        summed.reshape(EXPERTS, capacity, model_width), CHIP_AXES, 0, 0, tiled=True
    ).reshape(slots, model_width)
    routed = jnp.dot(combine_hi, returned, preferred_element_type=jnp.float32) + jnp.dot(
        combine_lo, returned, preferred_element_type=jnp.float32
    )
    hidden_out = (residual.astype(jnp.float32) + shared + routed).astype(jnp.bfloat16)
    return (hidden_out, latent_rows, own_rope)


def solution(mesh):
    chip_mesh = Mesh(
        mesh.devices.reshape(mesh.devices.shape[0], -1, 2), ("req",) + HEAD_AXES
    )
    placed = (
        P(("req",) + HEAD_AXES, None),
        P(),
        P(None, HEAD_AXES),
        P(),
        P(),
        P(),
        P(None, HEAD_AXES),
        P(HEAD_AXES, None),
        P("req", None, None),
        P("req", None, None),
        P("req", None),
        P("req"),
        P(),
        P(),
        P(("req",) + HEAD_AXES, None),
        P(None, None, HEAD_AXES),
        P(HEAD_AXES, None),
        P(("req",) + HEAD_AXES, None, None, None),
        P(("req",) + HEAD_AXES, None, None),
    )
    return jax.shard_map(
        body,
        mesh=chip_mesh,
        in_specs=placed,
        out_specs=(P(("req",) + HEAD_AXES, None), P(("req",) + HEAD_AXES, None), P(None, ("req",) + HEAD_AXES)),
        check_vma=False,
    )
```

```python
import math

import jax
import jax.numpy as jnp
from jax import lax
from jax.sharding import Mesh, PartitionSpec as P


HEAD_NOPE = 128
ROPE = 64
VDIM = 128
LATENT = 512
EXPERTS = 64
TOP = 6
HEAD_AXES = ("y", "core")
CHIP_AXES = ("req", "y")


EPSILON = 1e-06
THETA = 10000.0


def rms_norm(values, weights):
    widened = values.astype(jnp.float32)
    factor = lax.rsqrt(jnp.mean(widened * widened, axis=-1, keepdims=True) + EPSILON)
    return widened * factor * weights


def frequency_table(entries):
    return THETA ** (-2.0 * jnp.arange(entries // 2, dtype=jnp.float32) / entries)


def rotary_rows(values, places):
    halfway = values.shape[-1] // 2
    angles = places[:, None, None] * frequency_table(values.shape[-1])[None, None, :]
    cosine = jnp.cos(angles)
    sine_of = jnp.sin(angles)
    first_half = values[..., :halfway]
    second_half = values[..., halfway:]
    return jnp.concatenate(
        [first_half * cosine - second_half * sine_of, first_half * sine_of + second_half * cosine],
        axis=-1,
    )


def rotary_columns(values, places):
    halfway = values.shape[0] // 2
    angles = places[None, :] * frequency_table(values.shape[0])[:, None]
    cosine = jnp.cos(angles)
    sine_of = jnp.sin(angles)
    first_half = values[:halfway]
    second_half = values[halfway:]
    return jnp.concatenate(
        [first_half * cosine - second_half * sine_of, first_half * sine_of + second_half * cosine],
        axis=0,
    )


def body(
    hidden_in,
    attn_gain,
    query_weight,
    latent_weight,
    rope_key_weight,
    latent_gain,
    kv_up_weight,
    out_weight,
    pool_latent,
    pool_rope,
    page_table,
    cache_len,
    post_gain,
    router_weight,
    routes,
    shared_gate_up,
    shared_down,
    expert_gate_up,
    expert_down,
):
    swap = [(0, 1), (1, 0)]
    mate_gate_up = lax.ppermute(expert_gate_up, "core", swap)
    mate_down = lax.ppermute(expert_down, "core", swap)
    groups = lax.axis_size("y") * lax.axis_size("core")
    member = lax.axis_index("y") * lax.axis_size("core") + lax.axis_index("core")
    own_rows = hidden_in.shape[0]
    fresh_count = own_rows * groups
    model_width = hidden_in.shape[1]
    head_width = HEAD_NOPE + ROPE
    local_heads = query_weight.shape[1] // head_width
    length = cache_len[0]
    own_start = member * own_rows
    offsets = jnp.arange(fresh_count, dtype=jnp.int32)
    places = (length + offsets).astype(jnp.float32)
    own_places = lax.dynamic_slice_in_dim(places, own_start, own_rows, 0)
    gathered = lax.all_gather(hidden_in, HEAD_AXES, axis=0, tiled=True)
    normed = rms_norm(gathered, attn_gain).astype(jnp.bfloat16)
    own_normed = lax.dynamic_slice_in_dim(normed, own_start, own_rows, 0)
    latent_raw = jnp.dot(own_normed, latent_weight, preferred_element_type=jnp.float32)
    latent_rows = rms_norm(latent_raw, latent_gain).astype(jnp.bfloat16)
    rope_raw = jnp.einsum(
        "rd,nd->rn", rope_key_weight, own_normed, preferred_element_type=jnp.float32
    )
    own_rope = rotary_columns(rope_raw, own_places).astype(jnp.bfloat16)
    fresh_latent, fresh_rope = (
        lax.all_gather(latent_rows, HEAD_AXES, axis=0, tiled=True),
        lax.all_gather(own_rope, HEAD_AXES, axis=1, tiled=True),
    )
    queries = jnp.dot(normed, query_weight, preferred_element_type=jnp.float32).reshape(
        fresh_count, local_heads, head_width
    )
    query_nope = queries[..., :HEAD_NOPE].astype(jnp.bfloat16)
    query_rope = rotary_rows(queries[..., HEAD_NOPE:], places).astype(jnp.bfloat16)
    scale_factor = float(head_width) ** (-0.5)

    def keys_of(keys_latent):
        keys_up = jnp.dot(keys_latent, kv_up_weight, preferred_element_type=jnp.float32).astype(
            jnp.bfloat16
        )
        return keys_up.reshape(keys_latent.shape[0], local_heads, HEAD_NOPE + VDIM)

    def score_block(keys_up, keys_rope):
        scores = jnp.einsum(
            "thc,khc->htk", query_nope, keys_up[..., :HEAD_NOPE], preferred_element_type=jnp.float32
        )
        scores = (
            scores
            + jnp.einsum("thc,ck->htk", query_rope, keys_rope, preferred_element_type=jnp.float32)
        ) * scale_factor
        return (scores, keys_up[..., HEAD_NOPE:])

    def accumulate(running, scores, allowed, values):
        totals, mixture = running
        weights = jnp.where(allowed, jnp.exp(scores), 0.0)
        mixture = mixture + jnp.einsum(
            "htk,khv->thv", weights.astype(jnp.bfloat16), values, preferred_element_type=jnp.float32
        )
        return (totals + jnp.sum(weights, axis=-1), mixture)

    table_row = page_table[0]
    cache_rows = pool_latent.shape[0] * pool_latent.shape[1]
    cached_latent = pool_latent[table_row].reshape(cache_rows, LATENT)
    cached_rope = jnp.transpose(pool_rope[table_row], (1, 0, 2)).reshape(ROPE, cache_rows)
    stride = math.gcd(cache_rows, 512)
    cached_up = keys_of(cached_latent)

    def cache_step(position, running):
        first_row = position * stride
        keys_up = lax.dynamic_slice_in_dim(cached_up, first_row, stride, 0)
        keys_rope = lax.dynamic_slice_in_dim(cached_rope, first_row, stride, 1)
        scores, values = score_block(keys_up, keys_rope)
        allowed = (first_row + jnp.arange(stride, dtype=jnp.int32) < length)[None, None, :]
        return accumulate(running, scores, allowed, values)

    start_state = (
        jnp.zeros((local_heads, fresh_count), jnp.float32),
        jnp.zeros((fresh_count, local_heads, VDIM), jnp.float32),
    )
    used_blocks = (length + stride - 1) // stride
    running = lax.fori_loop(0, used_blocks, cache_step, start_state)
    scores, values = score_block(keys_of(fresh_latent), fresh_rope)
    allowed = (offsets[None, :] <= offsets[:, None])[None]
    totals, mixture = accumulate(running, scores, allowed, values)
    attended = (
        (mixture / jnp.transpose(totals)[..., None])
        .astype(jnp.bfloat16)
        .reshape(fresh_count, local_heads * VDIM)
    )
    rows_block = attended
    attn_sum = lax.psum_scatter(
        jnp.dot(rows_block, out_weight, preferred_element_type=jnp.float32).astype(jnp.bfloat16),
        HEAD_AXES,
        scatter_dimension=0,
        tiled=True,
    ).astype(jnp.float32)
    residual = (hidden_in.astype(jnp.float32) + attn_sum).astype(jnp.bfloat16)
    post_own = rms_norm(residual, post_gain).astype(jnp.bfloat16)
    piece = lax.all_gather(post_own, HEAD_AXES, axis=0, tiled=True)
    gate_part = jnp.dot(piece, shared_gate_up[0], preferred_element_type=jnp.float32)
    up_part = jnp.dot(piece, shared_gate_up[1], preferred_element_type=jnp.float32)
    inner_rows = (jax.nn.silu(gate_part) * up_part).astype(jnp.bfloat16)
    rows_block = inner_rows
    shared = lax.psum_scatter(
        jnp.dot(rows_block, shared_down, preferred_element_type=jnp.float32).astype(jnp.bfloat16),
        HEAD_AXES,
        scatter_dimension=0,
        tiled=True,
    ).astype(jnp.float32)
    logits = jnp.dot(post_own, router_weight, preferred_element_type=jnp.float32)
    picker = routes[:, :, None] == jnp.arange(EXPERTS, dtype=jnp.int32)[None, None, :]
    chosen_logits = jnp.sum(jnp.where(picker, logits[:, None, :], 0.0), axis=-1)
    raised = jnp.exp(chosen_logits)
    gate_share = raised / jnp.sum(raised, axis=1, keepdims=True)
    capacity = -(-max(2, own_rows * 7 // 64) // 16) * 16
    slots = EXPERTS * capacity
    flat_routes = routes.reshape(own_rows * TOP)
    onehot = (flat_routes[:, None] == jnp.arange(EXPERTS, dtype=jnp.int32)[None, :]).astype(
        jnp.int32
    )
    slot_rank = jnp.sum((jnp.cumsum(onehot, axis=0, dtype=jnp.int32) - onehot) * onehot, axis=1)
    slot_id = (flat_routes * capacity + slot_rank).reshape(own_rows, TOP)
    picked = slot_id[:, :, None] == jnp.arange(slots, dtype=jnp.int32)[None, None, :]
    dispatch = jnp.any(picked, axis=1).astype(jnp.bfloat16)
    combine = jnp.sum(jnp.where(picked, gate_share[:, :, None], 0.0), axis=1)
    combine_hi = combine.astype(jnp.bfloat16)
    combine_lo = (combine - combine_hi.astype(jnp.float32)).astype(jnp.bfloat16)
    outgoing = jnp.einsum(
        "ts,td->sd", dispatch, post_own, preferred_element_type=jnp.float32
    ).astype(jnp.bfloat16)
    received = lax.all_to_all(
        outgoing.reshape(EXPERTS, capacity, model_width), CHIP_AXES, 0, 0, tiled=True
    )
    piece = received.reshape(slots, model_width)

    def expert_half(gate_up, down):
        gate_part = jnp.dot(piece, gate_up[0], preferred_element_type=jnp.float32)
        up_part = jnp.dot(piece, gate_up[1], preferred_element_type=jnp.float32)
        inner_expert = (jax.nn.silu(gate_part) * up_part).astype(jnp.bfloat16)
        return jnp.dot(inner_expert, down, preferred_element_type=jnp.float32).astype(
            jnp.bfloat16
        )

    summed = (
        expert_half(expert_gate_up[0], expert_down[0]).astype(jnp.float32)
        + expert_half(mate_gate_up[0], mate_down[0]).astype(jnp.float32)
    ).astype(jnp.bfloat16)
    returned = lax.all_to_all(
        summed.reshape(EXPERTS, capacity, model_width), CHIP_AXES, 0, 0, tiled=True
    ).reshape(slots, model_width)
    routed = jnp.dot(combine_hi, returned, preferred_element_type=jnp.float32) + jnp.dot(
        combine_lo, returned, preferred_element_type=jnp.float32
    )
    hidden_out = (residual.astype(jnp.float32) + shared + routed).astype(jnp.bfloat16)
    return (hidden_out, latent_rows, own_rope)


def solution(mesh):
    chip_mesh = Mesh(
        mesh.devices.reshape(mesh.devices.shape[0], -1, 2), ("req",) + HEAD_AXES
    )
    placed = (
        P(("req",) + HEAD_AXES, None),
        P(),
        P(None, HEAD_AXES),
        P(),
        P(),
        P(),
        P(None, HEAD_AXES),
        P(HEAD_AXES, None),
        P("req", None, None),
        P("req", None, None),
        P("req", None),
        P("req"),
        P(),
        P(),
        P(("req",) + HEAD_AXES, None),
        P(None, None, HEAD_AXES),
        P(HEAD_AXES, None),
        P(("req",) + HEAD_AXES, None, None, None),
        P(("req",) + HEAD_AXES, None, None),
    )
    return jax.shard_map(
        body,
        mesh=chip_mesh,
        in_specs=placed,
        out_specs=(P(("req",) + HEAD_AXES, None), P(("req",) + HEAD_AXES, None), P(None, ("req",) + HEAD_AXES)),
        check_vma=False,
    )
```

```python
import math

import jax
import jax.numpy as jnp
from jax import lax
from jax.sharding import Mesh, PartitionSpec as P


HEAD_NOPE = 128
ROPE = 64
VDIM = 128
LATENT = 512
EXPERTS = 64
TOP = 6
HEAD_AXES = ("y", "core")
CHIP_AXES = ("req", "y")


EPSILON = 1e-06
THETA = 10000.0


def rms_norm(values, weights):
    widened = values.astype(jnp.float32)
    factor = lax.rsqrt(jnp.mean(widened * widened, axis=-1, keepdims=True) + EPSILON)
    return widened * factor * weights


def frequency_table(entries):
    return THETA ** (-2.0 * jnp.arange(entries // 2, dtype=jnp.float32) / entries)


def rotary_rows(values, places):
    halfway = values.shape[-1] // 2
    angles = places[:, None, None] * frequency_table(values.shape[-1])[None, None, :]
    cosine = jnp.cos(angles)
    sine_of = jnp.sin(angles)
    first_half = values[..., :halfway]
    second_half = values[..., halfway:]
    return jnp.concatenate(
        [first_half * cosine - second_half * sine_of, first_half * sine_of + second_half * cosine],
        axis=-1,
    )


def rotary_columns(values, places):
    halfway = values.shape[0] // 2
    angles = places[None, :] * frequency_table(values.shape[0])[:, None]
    cosine = jnp.cos(angles)
    sine_of = jnp.sin(angles)
    first_half = values[:halfway]
    second_half = values[halfway:]
    return jnp.concatenate(
        [first_half * cosine - second_half * sine_of, first_half * sine_of + second_half * cosine],
        axis=0,
    )


def body(
    hidden_in,
    attn_gain,
    query_weight,
    latent_weight,
    rope_key_weight,
    latent_gain,
    kv_up_weight,
    out_weight,
    pool_latent,
    pool_rope,
    page_table,
    cache_len,
    post_gain,
    router_weight,
    routes,
    shared_gate_up,
    shared_down,
    expert_gate_up,
    expert_down,
):
    swap = [(0, 1), (1, 0)]
    mate_gate_up = lax.ppermute(expert_gate_up, "core", swap)
    mate_down = lax.ppermute(expert_down, "core", swap)
    groups = lax.axis_size("y") * lax.axis_size("core")
    member = lax.axis_index("y") * lax.axis_size("core") + lax.axis_index("core")
    own_rows = hidden_in.shape[0]
    fresh_count = own_rows * groups
    model_width = hidden_in.shape[1]
    head_width = HEAD_NOPE + ROPE
    local_heads = query_weight.shape[1] // head_width
    length = cache_len[0]
    own_start = member * own_rows
    offsets = jnp.arange(fresh_count, dtype=jnp.int32)
    places = (length + offsets).astype(jnp.float32)
    own_places = lax.dynamic_slice_in_dim(places, own_start, own_rows, 0)
    gathered = lax.all_gather(hidden_in, HEAD_AXES, axis=0, tiled=True)
    normed = rms_norm(gathered, attn_gain).astype(jnp.bfloat16)
    own_normed = lax.dynamic_slice_in_dim(normed, own_start, own_rows, 0)
    latent_raw = jnp.dot(own_normed, latent_weight, preferred_element_type=jnp.float32)
    latent_rows = rms_norm(latent_raw, latent_gain).astype(jnp.bfloat16)
    rope_raw = jnp.einsum(
        "rd,nd->rn", rope_key_weight, own_normed, preferred_element_type=jnp.float32
    )
    own_rope = rotary_columns(rope_raw, own_places).astype(jnp.bfloat16)
    fresh_latent, fresh_rope = (
        lax.all_gather(latent_rows, HEAD_AXES, axis=0, tiled=True),
        lax.all_gather(own_rope, HEAD_AXES, axis=1, tiled=True),
    )
    queries = jnp.dot(normed, query_weight, preferred_element_type=jnp.float32).reshape(
        fresh_count, local_heads, head_width
    )
    query_nope = queries[..., :HEAD_NOPE].astype(jnp.bfloat16)
    query_rope = rotary_rows(queries[..., HEAD_NOPE:], places).astype(jnp.bfloat16)
    scale_factor = float(head_width) ** (-0.5)

    def score_block(keys_latent, keys_rope):
        keys_up = jnp.dot(keys_latent, kv_up_weight, preferred_element_type=jnp.float32).astype(
            jnp.bfloat16
        )
        keys_up = keys_up.reshape(keys_latent.shape[0], local_heads, HEAD_NOPE + VDIM)
        scores = jnp.einsum(
            "thc,khc->htk", query_nope, keys_up[..., :HEAD_NOPE], preferred_element_type=jnp.float32
        )
        scores = (
            scores
            + jnp.einsum("thc,ck->htk", query_rope, keys_rope, preferred_element_type=jnp.float32)
        ) * scale_factor
        return (scores, keys_up[..., HEAD_NOPE:])

    def accumulate(running, scores, allowed, values):
        totals, mixture = running
        weights = jnp.where(allowed, jnp.exp(scores), 0.0)
        mixture = mixture + jnp.einsum(
            "htk,khv->thv", weights.astype(jnp.bfloat16), values, preferred_element_type=jnp.float32
        )
        return (totals + jnp.sum(weights, axis=-1), mixture)

    table_row = page_table[0]
    cache_rows = pool_latent.shape[0] * pool_latent.shape[1]
    cached_latent = pool_latent[table_row].reshape(cache_rows, LATENT)
    cached_rope = jnp.transpose(pool_rope[table_row], (1, 0, 2)).reshape(ROPE, cache_rows)
    stride = math.gcd(cache_rows, 512)

    def cache_step(position, running):
        first_row = position * stride
        keys_latent = lax.dynamic_slice_in_dim(cached_latent, first_row, stride, 0)
        keys_rope = lax.dynamic_slice_in_dim(cached_rope, first_row, stride, 1)
        scores, values = score_block(keys_latent, keys_rope)
        allowed = (first_row + jnp.arange(stride, dtype=jnp.int32) < length)[None, None, :]
        return accumulate(running, scores, allowed, values)

    start_state = (
        jnp.zeros((local_heads, fresh_count), jnp.float32),
        jnp.zeros((fresh_count, local_heads, VDIM), jnp.float32),
    )
    used_blocks = (length + stride - 1) // stride
    running = lax.fori_loop(0, used_blocks, cache_step, start_state)
    scores, values = score_block(fresh_latent, fresh_rope)
    allowed = (offsets[None, :] <= offsets[:, None])[None]
    totals, mixture = accumulate(running, scores, allowed, values)
    attended = (
        (mixture / jnp.transpose(totals)[..., None])
        .astype(jnp.bfloat16)
        .reshape(fresh_count, local_heads * VDIM)
    )
    chip_count = lax.axis_size("y")
    core_count = lax.axis_size("core")
    rows_block = jnp.transpose(
        attended.reshape(chip_count, core_count, own_rows, local_heads * VDIM), (1, 0, 2, 3)
    ).reshape(fresh_count, local_heads * VDIM)
    partial = jnp.dot(rows_block, out_weight, preferred_element_type=jnp.float32).astype(
        jnp.bfloat16
    )
    core_parts = lax.all_to_all(
        partial.reshape(core_count, chip_count * own_rows, model_width), "core", 0, 0, tiled=True
    )
    chip_part = jnp.sum(core_parts.astype(jnp.float32), axis=0).astype(jnp.bfloat16)
    attn_sum = lax.psum_scatter(chip_part, "y", scatter_dimension=0, tiled=True).astype(
        jnp.float32
    )
    residual = (hidden_in.astype(jnp.float32) + attn_sum).astype(jnp.bfloat16)
    post_own = rms_norm(residual, post_gain).astype(jnp.bfloat16)
    piece = lax.all_gather(post_own, HEAD_AXES, axis=0, tiled=True)
    gate_part = jnp.dot(piece, shared_gate_up[0], preferred_element_type=jnp.float32)
    up_part = jnp.dot(piece, shared_gate_up[1], preferred_element_type=jnp.float32)
    inner_rows = (jax.nn.silu(gate_part) * up_part).astype(jnp.bfloat16)
    rows_block = inner_rows
    shared = lax.psum_scatter(
        jnp.dot(rows_block, shared_down, preferred_element_type=jnp.float32).astype(jnp.bfloat16),
        HEAD_AXES,
        scatter_dimension=0,
        tiled=True,
    ).astype(jnp.float32)
    logits = jnp.dot(post_own, router_weight, preferred_element_type=jnp.float32)
    picker = routes[:, :, None] == jnp.arange(EXPERTS, dtype=jnp.int32)[None, None, :]
    chosen_logits = jnp.sum(jnp.where(picker, logits[:, None, :], 0.0), axis=-1)
    raised = jnp.exp(chosen_logits)
    gate_share = raised / jnp.sum(raised, axis=1, keepdims=True)
    capacity = -(-max(2, own_rows * 7 // 64) // 16) * 16
    slots = EXPERTS * capacity
    flat_routes = routes.reshape(own_rows * TOP)
    onehot = (flat_routes[:, None] == jnp.arange(EXPERTS, dtype=jnp.int32)[None, :]).astype(
        jnp.int32
    )
    slot_rank = jnp.sum((jnp.cumsum(onehot, axis=0, dtype=jnp.int32) - onehot) * onehot, axis=1)
    slot_id = (flat_routes * capacity + slot_rank).reshape(own_rows, TOP)
    picked = slot_id[:, :, None] == jnp.arange(slots, dtype=jnp.int32)[None, None, :]
    dispatch = jnp.any(picked, axis=1).astype(jnp.bfloat16)
    combine = jnp.sum(jnp.where(picked, gate_share[:, :, None], 0.0), axis=1)
    combine_hi = combine.astype(jnp.bfloat16)
    combine_lo = (combine - combine_hi.astype(jnp.float32)).astype(jnp.bfloat16)
    outgoing = jnp.einsum(
        "ts,td->sd", dispatch, post_own, preferred_element_type=jnp.float32
    ).astype(jnp.bfloat16)
    received = lax.all_to_all(
        outgoing.reshape(EXPERTS, capacity, model_width), CHIP_AXES, 0, 0, tiled=True
    )
    piece = received.reshape(slots, model_width)

    def expert_half(gate_up, down):
        gate_part = jnp.dot(piece, gate_up[0], preferred_element_type=jnp.float32)
        up_part = jnp.dot(piece, gate_up[1], preferred_element_type=jnp.float32)
        inner_expert = (jax.nn.silu(gate_part) * up_part).astype(jnp.bfloat16)
        return jnp.dot(inner_expert, down, preferred_element_type=jnp.float32).astype(
            jnp.bfloat16
        )

    summed = (
        expert_half(expert_gate_up[0], expert_down[0]).astype(jnp.float32)
        + expert_half(mate_gate_up[0], mate_down[0]).astype(jnp.float32)
    ).astype(jnp.bfloat16)
    returned = lax.all_to_all(
        summed.reshape(EXPERTS, capacity, model_width), CHIP_AXES, 0, 0, tiled=True
    ).reshape(slots, model_width)
    routed = jnp.dot(combine_hi, returned, preferred_element_type=jnp.float32) + jnp.dot(
        combine_lo, returned, preferred_element_type=jnp.float32
    )
    hidden_out = (residual.astype(jnp.float32) + shared + routed).astype(jnp.bfloat16)
    return (hidden_out, latent_rows, own_rope)


def solution(mesh):
    chip_mesh = Mesh(
        mesh.devices.reshape(mesh.devices.shape[0], -1, 2), ("req",) + HEAD_AXES
    )
    placed = (
        P(("req",) + HEAD_AXES, None),
        P(),
        P(None, HEAD_AXES),
        P(),
        P(),
        P(),
        P(None, HEAD_AXES),
        P(HEAD_AXES, None),
        P("req", None, None),
        P("req", None, None),
        P("req", None),
        P("req"),
        P(),
        P(),
        P(("req",) + HEAD_AXES, None),
        P(None, None, HEAD_AXES),
        P(HEAD_AXES, None),
        P(("req",) + HEAD_AXES, None, None, None),
        P(("req",) + HEAD_AXES, None, None),
    )
    return jax.shard_map(
        body,
        mesh=chip_mesh,
        in_specs=placed,
        out_specs=(P(("req",) + HEAD_AXES, None), P(("req",) + HEAD_AXES, None), P(None, ("req",) + HEAD_AXES)),
        check_vma=False,
    )
```

```python
import math

import jax
import jax.numpy as jnp
from jax import lax
from jax.sharding import Mesh, PartitionSpec as P


HEAD_NOPE = 128
ROPE = 64
VDIM = 128
LATENT = 512
EXPERTS = 64
TOP = 6
HEAD_AXES = ("y", "core")
CHIP_AXES = ("req", "y")


EPSILON = 1e-06
THETA = 10000.0


def rms_norm(values, weights):
    widened = values.astype(jnp.float32)
    factor = lax.rsqrt(jnp.mean(widened * widened, axis=-1, keepdims=True) + EPSILON)
    return widened * factor * weights


def frequency_table(entries):
    return THETA ** (-2.0 * jnp.arange(entries // 2, dtype=jnp.float32) / entries)


def rotary_rows(values, places):
    halfway = values.shape[-1] // 2
    angles = places[:, None, None] * frequency_table(values.shape[-1])[None, None, :]
    cosine = jnp.cos(angles)
    sine_of = jnp.sin(angles)
    first_half = values[..., :halfway]
    second_half = values[..., halfway:]
    return jnp.concatenate(
        [first_half * cosine - second_half * sine_of, first_half * sine_of + second_half * cosine],
        axis=-1,
    )


def rotary_columns(values, places):
    halfway = values.shape[0] // 2
    angles = places[None, :] * frequency_table(values.shape[0])[:, None]
    cosine = jnp.cos(angles)
    sine_of = jnp.sin(angles)
    first_half = values[:halfway]
    second_half = values[halfway:]
    return jnp.concatenate(
        [first_half * cosine - second_half * sine_of, first_half * sine_of + second_half * cosine],
        axis=0,
    )


def body(
    hidden_in,
    attn_gain,
    query_weight,
    latent_weight,
    rope_key_weight,
    latent_gain,
    kv_up_weight,
    out_weight,
    pool_latent,
    pool_rope,
    page_table,
    cache_len,
    post_gain,
    router_weight,
    routes,
    shared_gate_up,
    shared_down,
    expert_gate_up,
    expert_down,
):
    swap = [(0, 1), (1, 0)]
    mate_gate_up = lax.ppermute(expert_gate_up, "core", swap)
    mate_down = lax.ppermute(expert_down, "core", swap)
    groups = lax.axis_size("y") * lax.axis_size("core")
    member = lax.axis_index("y") * lax.axis_size("core") + lax.axis_index("core")
    own_rows = hidden_in.shape[0]
    fresh_count = own_rows * groups
    model_width = hidden_in.shape[1]
    head_width = HEAD_NOPE + ROPE
    local_heads = query_weight.shape[1] // head_width
    length = cache_len[0]
    own_start = member * own_rows
    offsets = jnp.arange(fresh_count, dtype=jnp.int32)
    places = (length + offsets).astype(jnp.float32)
    own_places = lax.dynamic_slice_in_dim(places, own_start, own_rows, 0)
    gathered = lax.all_gather(hidden_in, HEAD_AXES, axis=0, tiled=True)
    normed = rms_norm(gathered, attn_gain).astype(jnp.bfloat16)
    own_normed = lax.dynamic_slice_in_dim(normed, own_start, own_rows, 0)
    latent_raw = jnp.dot(own_normed, latent_weight, preferred_element_type=jnp.float32)
    latent_rows = rms_norm(latent_raw, latent_gain).astype(jnp.bfloat16)
    rope_raw = jnp.einsum(
        "rd,nd->rn", rope_key_weight, own_normed, preferred_element_type=jnp.float32
    )
    own_rope = rotary_columns(rope_raw, own_places).astype(jnp.bfloat16)
    lane_pad = -ROPE % 128
    packed = jnp.concatenate(
        [latent_rows, jnp.transpose(own_rope), jnp.zeros((own_rows, lane_pad), jnp.bfloat16)],
        axis=1,
    )
    fresh_keys = lax.all_gather(packed, HEAD_AXES, axis=0, tiled=True)
    fresh_latent = fresh_keys[:, :LATENT]
    fresh_rope = jnp.transpose(fresh_keys[:, LATENT:LATENT + ROPE])
    queries = jnp.dot(normed, query_weight, preferred_element_type=jnp.float32).reshape(
        fresh_count, local_heads, head_width
    )
    query_nope = queries[..., :HEAD_NOPE].astype(jnp.bfloat16)
    query_rope = rotary_rows(queries[..., HEAD_NOPE:], places).astype(jnp.bfloat16)
    scale_factor = float(head_width) ** (-0.5)

    def score_block(keys_latent, keys_rope):
        keys_up = jnp.dot(keys_latent, kv_up_weight, preferred_element_type=jnp.float32).astype(
            jnp.bfloat16
        )
        keys_up = keys_up.reshape(keys_latent.shape[0], local_heads, HEAD_NOPE + VDIM)
        scores = jnp.einsum(
            "thc,khc->htk", query_nope, keys_up[..., :HEAD_NOPE], preferred_element_type=jnp.float32
        )
        scores = (
            scores
            + jnp.einsum("thc,ck->htk", query_rope, keys_rope, preferred_element_type=jnp.float32)
        ) * scale_factor
        return (scores, keys_up[..., HEAD_NOPE:])

    def accumulate(running, scores, allowed, values):
        totals, mixture = running
        weights = jnp.where(allowed, jnp.exp(scores), 0.0)
        mixture = mixture + jnp.einsum(
            "htk,khv->thv", weights.astype(jnp.bfloat16), values, preferred_element_type=jnp.float32
        )
        return (totals + jnp.sum(weights, axis=-1), mixture)

    table_row = page_table[0]
    cache_rows = pool_latent.shape[0] * pool_latent.shape[1]
    cached_latent = pool_latent[table_row].reshape(cache_rows, LATENT)
    cached_rope = jnp.transpose(pool_rope[table_row], (1, 0, 2)).reshape(ROPE, cache_rows)
    stride = math.gcd(cache_rows, 512)

    def cache_step(position, running):
        first_row = position * stride
        keys_latent = lax.dynamic_slice_in_dim(cached_latent, first_row, stride, 0)
        keys_rope = lax.dynamic_slice_in_dim(cached_rope, first_row, stride, 1)
        scores, values = score_block(keys_latent, keys_rope)
        allowed = (first_row + jnp.arange(stride, dtype=jnp.int32) < length)[None, None, :]
        return accumulate(running, scores, allowed, values)

    start_state = (
        jnp.zeros((local_heads, fresh_count), jnp.float32),
        jnp.zeros((fresh_count, local_heads, VDIM), jnp.float32),
    )
    used_blocks = (length + stride - 1) // stride
    running = lax.fori_loop(0, used_blocks, cache_step, start_state)
    scores, values = score_block(fresh_latent, fresh_rope)
    allowed = (offsets[None, :] <= offsets[:, None])[None]
    totals, mixture = accumulate(running, scores, allowed, values)
    attended = (
        (mixture / jnp.transpose(totals)[..., None])
        .astype(jnp.bfloat16)
        .reshape(fresh_count, local_heads * VDIM)
    )
    rows_block = attended
    attn_sum = lax.psum_scatter(
        jnp.dot(rows_block, out_weight, preferred_element_type=jnp.float32).astype(jnp.bfloat16),
        HEAD_AXES,
        scatter_dimension=0,
        tiled=True,
    ).astype(jnp.float32)
    residual = (hidden_in.astype(jnp.float32) + attn_sum).astype(jnp.bfloat16)
    post_own = rms_norm(residual, post_gain).astype(jnp.bfloat16)
    piece = lax.all_gather(post_own, HEAD_AXES, axis=0, tiled=True)
    gate_part = jnp.dot(piece, shared_gate_up[0], preferred_element_type=jnp.float32)
    up_part = jnp.dot(piece, shared_gate_up[1], preferred_element_type=jnp.float32)
    inner_rows = (jax.nn.silu(gate_part) * up_part).astype(jnp.bfloat16)
    rows_block = inner_rows
    shared = lax.psum_scatter(
        jnp.dot(rows_block, shared_down, preferred_element_type=jnp.float32).astype(jnp.bfloat16),
        HEAD_AXES,
        scatter_dimension=0,
        tiled=True,
    ).astype(jnp.float32)
    logits = jnp.dot(post_own, router_weight, preferred_element_type=jnp.float32)
    picker = routes[:, :, None] == jnp.arange(EXPERTS, dtype=jnp.int32)[None, None, :]
    chosen_logits = jnp.sum(jnp.where(picker, logits[:, None, :], 0.0), axis=-1)
    raised = jnp.exp(chosen_logits)
    gate_share = raised / jnp.sum(raised, axis=1, keepdims=True)
    capacity = -(-max(2, own_rows * 7 // 64) // 16) * 16
    slots = EXPERTS * capacity
    flat_routes = routes.reshape(own_rows * TOP)
    onehot = (flat_routes[:, None] == jnp.arange(EXPERTS, dtype=jnp.int32)[None, :]).astype(
        jnp.int32
    )
    slot_rank = jnp.sum((jnp.cumsum(onehot, axis=0, dtype=jnp.int32) - onehot) * onehot, axis=1)
    slot_id = (flat_routes * capacity + slot_rank).reshape(own_rows, TOP)
    picked = slot_id[:, :, None] == jnp.arange(slots, dtype=jnp.int32)[None, None, :]
    dispatch = jnp.any(picked, axis=1).astype(jnp.bfloat16)
    combine = jnp.sum(jnp.where(picked, gate_share[:, :, None], 0.0), axis=1)
    combine_hi = combine.astype(jnp.bfloat16)
    combine_lo = (combine - combine_hi.astype(jnp.float32)).astype(jnp.bfloat16)
    outgoing = jnp.einsum(
        "ts,td->sd", dispatch, post_own, preferred_element_type=jnp.float32
    ).astype(jnp.bfloat16)
    received = lax.all_to_all(
        outgoing.reshape(EXPERTS, capacity, model_width), CHIP_AXES, 0, 0, tiled=True
    )
    piece = received.reshape(slots, model_width)

    def expert_half(gate_up, down):
        gate_part = jnp.dot(piece, gate_up[0], preferred_element_type=jnp.float32)
        up_part = jnp.dot(piece, gate_up[1], preferred_element_type=jnp.float32)
        inner_expert = (jax.nn.silu(gate_part) * up_part).astype(jnp.bfloat16)
        return jnp.dot(inner_expert, down, preferred_element_type=jnp.float32).astype(
            jnp.bfloat16
        )

    summed = (
        expert_half(expert_gate_up[0], expert_down[0]).astype(jnp.float32)
        + expert_half(mate_gate_up[0], mate_down[0]).astype(jnp.float32)
    ).astype(jnp.bfloat16)
    returned = lax.all_to_all(
        summed.reshape(EXPERTS, capacity, model_width), CHIP_AXES, 0, 0, tiled=True
    ).reshape(slots, model_width)
    routed = jnp.dot(combine_hi, returned, preferred_element_type=jnp.float32) + jnp.dot(
        combine_lo, returned, preferred_element_type=jnp.float32
    )
    hidden_out = (residual.astype(jnp.float32) + shared + routed).astype(jnp.bfloat16)
    return (hidden_out, latent_rows, own_rope)


def solution(mesh):
    chip_mesh = Mesh(
        mesh.devices.reshape(mesh.devices.shape[0], -1, 2), ("req",) + HEAD_AXES
    )
    placed = (
        P(("req",) + HEAD_AXES, None),
        P(),
        P(None, HEAD_AXES),
        P(),
        P(),
        P(),
        P(None, HEAD_AXES),
        P(HEAD_AXES, None),
        P("req", None, None),
        P("req", None, None),
        P("req", None),
        P("req"),
        P(),
        P(),
        P(("req",) + HEAD_AXES, None),
        P(None, None, HEAD_AXES),
        P(HEAD_AXES, None),
        P(("req",) + HEAD_AXES, None, None, None),
        P(("req",) + HEAD_AXES, None, None),
    )
    return jax.shard_map(
        body,
        mesh=chip_mesh,
        in_specs=placed,
        out_specs=(P(("req",) + HEAD_AXES, None), P(("req",) + HEAD_AXES, None), P(None, ("req",) + HEAD_AXES)),
        check_vma=False,
    )
```
